32 devices in a mesh: strat: 4 (over z), rep: 8 (over y, x, core).
Axes of the slice: x: 2, y: 2, z: 4, core: 2. Of those that a mesh axis runs over, the one named last changes fastest.
Arguments:
- ratings: bfloat16 [128, 128, 128], P(('strat', 'rep')), may hold values from -6 to 6
- row_mask: int32 [128, 128], P(('strat', 'rep')), may hold values 0 or 1
- tile_owner: int32 [128, 1], P(('strat', 'rep')), may hold values from 0 to 3; in each aligned block of 4 rows (0 to 3, 4 to 7, ...) at most 2 rows name the same one
- tile_row: int32 [128], P(('strat', 'rep')), may hold values from 0 to 3
- tile_col: int32 [128], P(('strat', 'rep')), may hold values from 0 to 1
- tile_count: int32 [32], P(('strat', 'rep')), may hold values from 2 to 4, as said below
- row_factors: bfloat16 [2048, 256], P(('strat', 'rep')), may hold values from -1.5 to 1.5
- col_factors: bfloat16 [8192, 256], P(('strat', 'rep')), may hold values from -1.5 to 1.5
Outputs:
- row_grad: float32 [2048, 256], P(('strat', 'rep'))
- col_grad: float32 [8192, 256], P(('strat', 'rep'))
The draws below stay inside these ranges and needn't reach their ends.
Inputs may be any that keep to these rules, and one draw needn't show every extreme that they name: `tile_owner`: among the 4 slots of one device at most 2 name the same owner, and on some device exactly 2 do. `tile_count`: some device holds 4 live tiles.
All inputs are finite; a program needn't handle non-finite values. No bound on the sum of `row_mask` on one device may be relied on, other than what follows from the above.
Results may differ from the reference program's by a relative error of at most 0.0016.
Values may be sent and summed in bfloat16 or wider, within the bound.
A program may use at most 64 MiB of HBM per device.

```python
import math
import jax
import jax.numpy as jnp
import numpy as np
from jax import lax

K = 256
TILE = 128
CAP = 2
RB_DEV = 4
CB_DEV = 2
TILES_DEV = 4
ALL_TILES = 128
U_ROWS = 2048
V_ROWS = 8192
N_STRAT = 4
N_REP = 8


def draw_tile_count(key, part):
    count_key, pick_key = jax.random.split(jax.random.fold_in(key, 17))
    devices_all = N_STRAT * N_REP
    counts_drawn = jax.random.randint(count_key, (devices_all,), TILES_DEV // 2, TILES_DEV + 1)
    chosen = jax.random.randint(pick_key, (), 0, devices_all)
    positions = jnp.arange(devices_all, dtype=jnp.int32)
    return jnp.where(positions == chosen, TILES_DEV, counts_drawn).astype(jnp.int32)


def place_ends(result, own_key, least, high):
    longest = result.shape.index(max(result.shape))
    spots = []
    for shift in (0, 1):
        where = [jax.random.randint(jax.random.fold_in(own_key, axis), (), 0, length) for axis, length in enumerate(result.shape)]
        where[longest] = (where[longest] + shift) % result.shape[longest]
        spots.append(tuple(where))
    return result.at[spots[0]].set(least).at[spots[1]].set(high)


def steps_of(own_key, shape, shards, least, largest):
    def one(position, parts):
        heights = jax.random.uniform(jax.random.fold_in(jax.random.fold_in(own_key, 6), position), (parts,), jnp.float32, least / len(shards), largest / len(shards))
        return jnp.repeat(jnp.exp(heights), shape[position] // parts).reshape((-1,) + (1,) * (len(shape) - position - 1))

    loudness = one(*shards[0])
    for cut in shards[1:]:
        loudness = loudness * one(*cut)
    return loudness


def routed_block(own_key, own, number, rows, count, top, bound, skew):
    sequence = jax.random.permutation(own_key, count)
    packed, ordinary = portions_of(count, rows * top, bound, skew, True), portions_of(count, rows * top, bound, skew, False)
    places = jnp.arange(count)

    def named(sizes, rotation):
        used = int((sizes > 0).sum())
        fixed = max(1, used // 4)
        shifted = fixed + (places - fixed + rotation * (used - fixed)) % max(1, count - fixed)
        return jnp.zeros((count,), jnp.int32).at[sequence[jnp.where(places < fixed, places, shifted)]].set(jnp.asarray(sizes, jnp.int32))

    sizes = jnp.where(number % 4 == 0, named(packed, number // 4), named(ordinary, number - number // 4 - 1))
    mixed = jax.random.permutation(jax.random.fold_in(own, 3), count)
    donor, receiver = mixed[0:count // 2 * 2:2], mixed[1:count // 2 * 2:2]
    margin = jnp.minimum(sizes[donor] - 1, bound - sizes[receiver]) // 2
    margin = jnp.where((donor == sequence[0]) | (receiver == sequence[0]) | (sizes[receiver] == 0), 0, jnp.maximum(margin, 0))
    shifted = jax.random.randint(jax.random.fold_in(own, 4), (count // 2,), 0, 1 << 20) % (margin + 1)
    sizes = sizes.at[donor].add(-shifted).at[receiver].add(shifted)
    labels = jnp.searchsorted(jnp.cumsum(sizes), jnp.arange(rows * top), side="right").astype(jnp.int32)
    grid = labels.reshape(top, rows).T
    grid = grid[jax.random.permutation(jax.random.fold_in(own, 1), rows)]
    rotation = jax.random.randint(jax.random.fold_in(own, 2), (rows, 1), 0, top)
    return jnp.take_along_axis(grid, (jnp.arange(top)[None, :] + rotation) % top, axis=1)


def portions_of(count, total, reach, slope, full):
    weights = [(1 << 20) // math.isqrt(rank ** slope) + 1 for rank in range(1, count + 1)]
    largest = reach if full else min(reach, max(-(-total // count), total * weights[0] // sum(weights)))
    least = 1 if total - largest >= count - 1 else 0
    holding, spare = [largest] + [least] * (count - 1), total - largest - least * (count - 1)
    while spare > 0:
        candidates = [i for i in range(1, count) if holding[i] < largest] or [i for i in range(1, count) if holding[i] < reach]
        pool, left = sum([weights[i] for i in candidates]), spare
        for i in candidates:
            extra = min(reach - holding[i], max(1, left * weights[i] // pool), spare)
            holding[i] = holding[i] + extra
            spare = spare - extra
    return np.array(holding)


def bell_draw(stream_key, dims, spread, bound, cuts=(), kind=jnp.bfloat16):
    entries = spread * jax.random.normal(stream_key, dims, jnp.float32)
    if cuts:
        entries = entries * steps_of(stream_key, dims, cuts, -0.22, 0.18)
    return jnp.clip(entries, -bound, bound).astype(kind)


def setup_inputs(seed: int = 0) -> dict:
    keys = jax.random.split(jax.random.key(seed), 9)
    ratings = bell_draw(keys[0], (ALL_TILES, TILE, TILE), 1.0, 6.0, ((0, 32),))
    row_mask = place_ends((jax.random.randint(keys[1], (ALL_TILES, TILE), 0, 5) < 3).astype(jnp.int32), jax.random.fold_in(keys[1], 1), 0, 1)
    tile_owner_keys = jax.random.split(jax.random.fold_in(keys[2], 1), ALL_TILES // TILES_DEV)
    tile_owner_turns = jax.random.permutation(jax.random.fold_in(keys[2], 3), ALL_TILES // TILES_DEV)
    tile_owner = jax.vmap(lambda own, number: routed_block(jax.random.fold_in(keys[2], 2), own, number, TILES_DEV, N_STRAT, 1, CAP, 2))(tile_owner_keys, tile_owner_turns).reshape((ALL_TILES, 1))
    tile_row = place_ends(jax.random.randint(keys[3], (ALL_TILES,), 0, RB_DEV), jax.random.fold_in(keys[3], 1), 0, RB_DEV - 1).astype(jnp.int32)
    tile_col = place_ends(jax.random.randint(keys[4], (ALL_TILES,), 0, CB_DEV), jax.random.fold_in(keys[4], 1), 0, CB_DEV - 1).astype(jnp.int32)
    tile_count = draw_tile_count(jax.random.fold_in(keys[8], 71), 0)
    row_factors = bell_draw(keys[6], (U_ROWS, K), 16 ** -0.5, 1.5, ((0, 32),))
    col_factors = bell_draw(keys[7], (V_ROWS, K), 16 ** -0.5, 1.5, ((0, 32),))
    return dict(ratings=ratings, row_mask=row_mask, tile_owner=tile_owner, tile_row=tile_row, tile_col=tile_col, tile_count=tile_count, row_factors=row_factors, col_factors=col_factors)


def reference(ratings, row_mask, tile_owner, tile_row, tile_col, tile_count, row_factors, col_factors):
    device_total = N_STRAT * N_REP
    row_blocks = row_factors.reshape(N_STRAT * RB_DEV, TILE, K)
    col_blocks = col_factors.reshape(device_total * CB_DEV, TILE, K)
    tile_values = ratings.reshape(device_total, TILES_DEV, TILE, TILE)
    tile_masks = row_mask.reshape(device_total, TILES_DEV, TILE)
    owners = tile_owner.reshape(device_total, TILES_DEV)
    row_ids = tile_row.reshape(device_total, TILES_DEV)
    col_ids = tile_col.reshape(device_total, TILES_DEV)
    device_ids = jnp.arange(device_total, dtype=jnp.int32)

    def advance(carry, inputs_now):
        row_accum, col_accum = carry
        device_index, values, masks, owner_now, row_now, col_now, live_count = inputs_now
        is_live = (jnp.arange(TILES_DEV, dtype=jnp.int32) < live_count).astype(jnp.float32)
        rep_index = device_index % N_REP
        row_index = (owner_now * RB_DEV + row_now).astype(jnp.int32)
        col_index = ((owner_now * N_REP + rep_index) * CB_DEV + col_now).astype(jnp.int32)
        row_pick = row_blocks[row_index].astype(jnp.float32)
        col_pick = col_blocks[col_index].astype(jnp.float32)
        predicted = jnp.einsum("sik,sjk->sij", row_pick, col_pick)
        keep_rows = masks.astype(jnp.float32) * is_live[:, None]
        errors = keep_rows[:, :, None] * (predicted - values.astype(jnp.float32))
        errors = lax.optimization_barrier(errors.astype(jnp.bfloat16)).astype(jnp.float32)
        row_terms = jnp.einsum("sij,sjk->sik", errors, col_pick) * 0.0625
        col_terms = jnp.einsum("sij,sik->sjk", errors, row_pick) * 0.0625
        row_accum = row_accum.at[row_index].add(row_terms)
        col_accum = col_accum.at[col_index].add(col_terms)
        return (row_accum, col_accum), None

    start = (jnp.zeros((N_STRAT * RB_DEV, TILE, K), jnp.float32),
             jnp.zeros((device_total * CB_DEV, TILE, K), jnp.float32))
    (row_accum, col_accum), _ = lax.scan(
        advance, start,
        (device_ids, tile_values, tile_masks, owners, row_ids, col_ids, tile_count))
    return row_accum.reshape(U_ROWS, K), col_accum.reshape(V_ROWS, K)
```

```python
import functools

import jax
import jax.numpy as jnp
from jax import lax
from jax.experimental import pallas as pl
from jax.experimental.pallas import tpu as pltpu
from jax.sharding import PartitionSpec as P

CAP = 2


grad_scale = 0.0625
MESH = pl.DeviceIdType.MESH


def remote(src, dst, send_sem, recv_sem, **where):
    return pltpu.make_async_remote_copy(
        src_ref=src,
        dst_ref=dst,
        send_sem=send_sem,
        recv_sem=recv_sem,
        device_id=where,
        device_id_type=MESH,
    )


def kernel(
    n_strat, n_rep,
    owner_in, tile_row_in, tile_col_in, count_in, ratings, row_mask, row_factors, col_factors,
    row_out, col_out,
    owner, tile_row, tile_col, count,
    tiles, masks, row_all, col_all, send_vals, send_meta, recv_vals, recv_meta,
    row_acc, row_send, col_errors, row_picks, land_pair, land_far,
    predictions, keeps, col_picks,
    small_sem, local_sem, u_send, u_recv, v_send, v_recv, m_send, m_recv,
    p_send, p_recv, d_send, d_recv, ready,
):
    held, edge = tiles.shape[0], tiles.shape[1]
    rows = row_factors.shape[0]
    n_row, n_col = row_all.shape[0] // edge, col_all.shape[0] // edge
    me_s, me_q = lax.axis_index("strat"), lax.axis_index("rep")
    pairs = n_rep // 2
    chip, side = me_q // 2, lax.rem(me_q, 2)
    partner = 2 * chip + 1 - side
    peers, own = n_strat - 1, n_strat - 1

    def rows_of(index):
        return pl.ds(pl.multiple_of(index * rows, rows), rows)

    def other(k, me):
        past = jnp.where(k >= me, 1, 0)
        return k + past, me - 1 + past

    def pick(blocks, same):
        wide = blocks.shape[1] // edge
        chosen = None
        for b, flag in enumerate(same):
            flag = jnp.concatenate([flag] * wide, axis=1)
            weight = jnp.broadcast_to(flag, (edge, wide * edge)).astype(blocks.dtype)
            part = blocks[b * edge : (b + 1) * edge, :] * weight
            chosen = part if chosen is None else chosen + part
        return chosen

    local = [
        pltpu.make_async_copy(row_mask, masks, local_sem.at[0]),
        pltpu.make_async_copy(ratings, tiles, local_sem.at[1]),
        pltpu.make_async_copy(row_factors, row_all.at[rows_of(me_q)], local_sem.at[2]),
        pltpu.make_async_copy(col_factors, col_all, local_sem.at[3]),
    ]
    small = [
        pltpu.make_async_copy(source, target, small_sem.at[i])
        for i, (source, target) in enumerate(
            [(owner_in, owner), (tile_row_in, tile_row), (tile_col_in, tile_col), (count_in, count)]
        )
    ]
    for copy in small + local[:2]:
        copy.start()

    barrier = pltpu.get_barrier_semaphore()
    for k in range(peers):
        pl.semaphore_signal(
            barrier, inc=1, device_id={"strat": other(k, me_s)[0], "rep": 2 * chip},
            device_id_type=MESH,
        )
    for k in range(pairs - 1):
        pl.semaphore_signal(
            barrier, inc=1, device_id={"rep": 2 * other(k, chip)[0] + 1}, device_id_type=MESH
        )
    pl.semaphore_signal(barrier, inc=1, device_id={"rep": partner}, device_id_type=MESH)
    for copy in local[2:]:
        copy.start()

    for copy in small:
        copy.wait()

    live = [p < count[0, 0] for p in range(held)]
    owners = [owner[p] for p in range(held)]
    plan = []
    for k in range(n_strat):
        dest = me_s if k == own else other(k, me_s)[0]
        seen = jnp.int32(0)
        flags = [[] for _ in range(CAP)]
        slot_ids = [[jnp.int32(0), jnp.int32(0)] for _ in range(CAP)]
        for p in range(held):
            here = jnp.where(jnp.logical_and(live[p], owners[p] == dest), 1, 0)
            for i in range(CAP):
                flag = jnp.where(seen == i, here, 0)
                flags[i].append(flag)
                slot_ids[i][0] += flag * tile_row[p]
                slot_ids[i][1] += flag * tile_col[p]
            seen = seen + here
        plan.append((flags, slot_ids))

    local[0].wait()
    for k in range(n_strat):
        flags, slot_ids = plan[k]
        meta = recv_meta.at[own] if k == own else send_meta.at[k]
        for i in range(CAP):
            row = masks[0:1, :] * flags[i][0]
            for p in range(1, held):
                row = row + masks[p : p + 1, :] * flags[i][p]
            meta[i : i + 1, :] = row
            for j in range(2):
                at = (1 + j) * CAP + i
                meta[at : at + 1, :] = jnp.full((1, edge), slot_ids[i][j], jnp.int32)
        meta[3 * CAP :, :] = jnp.zeros((meta.shape[0] - 3 * CAP, edge), jnp.int32)
    local[1].wait()
    for k in range(n_strat):
        flags, _ = plan[k]
        slots = recv_vals.at[own] if k == own else send_vals.at[k]
        for i in range(CAP):
            value = None
            for p in range(held):
                weight = jnp.full((edge, edge), flags[i][p].astype(jnp.float32)).astype(tiles.dtype)
                part = tiles[p] * weight
                value = part if value is None else value + part
            slots[i] = value

    m_copies, v_copies = [], []
    for k in range(peers):
        dest, slot = other(k, me_s)
        m_copies.append(
            remote(send_meta.at[k], recv_meta.at[slot], m_send.at[k], m_recv.at[slot], strat=dest)
        )
        v_copies.append(
            remote(send_vals.at[k], recv_vals.at[slot], v_send.at[k], v_recv.at[slot], strat=dest)
        )
    far = [(k, e) for k in range(pairs - 1) for e in range(2)]

    def far_peer(k, e):
        target, slot = other(k, chip)
        return 2 * target + lax.rem(side + e, 2), 2 * slot + e

    u_copies = []
    for i, (k, e) in enumerate(far):
        peer, slot = far_peer(k, e)
        u_copies.append(
            remote(row_factors, row_all.at[rows_of(me_q)], u_send.at[i], u_recv.at[slot], rep=peer)
        )
    u_copies.append(
        remote(
            row_factors, row_all.at[rows_of(me_q)], u_send.at[len(far)], u_recv.at[len(far)],
            rep=partner,
        )
    )

    def meet(is_mine, count):
        @pl.when(is_mine)
        def _():
            pl.semaphore_wait(barrier, count)
            pl.semaphore_signal(ready, inc=1, device_id={"rep": partner}, device_id_type=MESH)

        @pl.when(jnp.logical_not(is_mine))
        def _():
            pl.semaphore_wait(ready, 1)

    def send_rows():
        meet(side == 1, n_rep - 1)
        for copy in u_copies:
            copy.start()

    def send_tiles():
        meet(side == 0, 2 * peers + 1)
        for copy in m_copies + v_copies:
            copy.start()

    rows_first = 2 * me_s < n_strat

    @pl.when(rows_first)
    def _():
        send_rows()
        send_tiles()

    @pl.when(jnp.logical_not(rows_first))
    def _():
        send_tiles()
        send_rows()

    order = [own] + list(range(peers))

    def arrived(copy_of, slot):
        copy_of(slot).wait_recv()

    def m_at(slot):
        return remote(
            send_meta.at[slot], recv_meta.at[slot], m_send.at[slot], m_recv.at[slot],
            strat=other(slot, me_s)[0],
        )

    def v_at(slot):
        return remote(
            send_vals.at[slot], recv_vals.at[slot], v_send.at[slot], v_recv.at[slot],
            strat=other(slot, me_s)[0],
        )

    def u_at(slot):
        return remote(
            row_factors, row_all.at[rows_of(me_q)], u_send.at[slot], u_recv.at[slot], rep=partner
        )

    for k in range(peers):
        m_at(k).wait_recv()
    local[2].wait()
    local[3].wait()
    for i in range(n_rep - 1):
        u_at(i).wait_recv()

    def flags_of(r):
        meta = recv_meta[r].astype(jnp.float32)
        in_row, in_col = [], []
        for k in range(CAP):
            row_id, col_id = (meta[(1 + i) * CAP + k : (1 + i) * CAP + k + 1, :] for i in range(2))
            in_row.append([jnp.where(row_id == b, 1.0, 0.0) for b in range(n_row)])
            in_col.append([jnp.where(col_id == c, 1.0, 0.0) for c in range(n_col)])
        return meta, in_row, in_col

    for r in order:
        meta, in_row, in_col = flags_of(r)
        keep = meta.T
        for k in range(CAP):
            row_pick, col_pick = pick(row_all, in_row[k]), pick(col_all, in_col[k])
            row_picks[r, k * edge : (k + 1) * edge, :] = row_pick
            col_picks[r, k * edge : (k + 1) * edge, :] = col_pick
            predictions[r, k] = lax.dot_general(
                row_pick, col_pick, (((1,), (1,)), ((), ())), preferred_element_type=jnp.float32
            )
            keeps[r, k] = jnp.broadcast_to(keep[:, k : k + 1], (edge, edge))

    def add_columns(r, scale):
        term = lax.dot_general(
            col_errors[r], row_picks[r], (((0,), (0,)), ((), ())),
            preferred_element_type=jnp.float32,
        )
        if r != order[0]:
            term = col_out[...] + term
        col_out[...] = term * scale

    for r in order:
        _, row_same, in_col = flags_of(r)
        if r != own:
            v_at(r).wait_recv()
        errors = []
        for k in range(CAP):
            error = keeps[r, k] * (predictions[r, k] - recv_vals[r, k].astype(jnp.float32))
            errors.append(error)
            for c in range(n_col):
                col_errors[r, k * edge : (k + 1) * edge, c * edge : (c + 1) * edge] = (
                    error * in_col[k][c]
                ).astype(jnp.bfloat16)
        stacked = col_picks[r]
        for b in range(n_row):
            left = jnp.concatenate(
                [
                    (errors[k] * row_same[k][b]).astype(jnp.bfloat16)
                    for k in range(CAP)
                ],
                axis=1,
            )
            term = jnp.dot(left, stacked, preferred_element_type=jnp.float32)
            block = slice(b * edge, (b + 1) * edge)
            if r != order[0]:
                term = row_acc[block, :] + term
            row_acc[block, :] = term
            if r == order[-1]:
                row_send[block, :] = term.astype(row_send.dtype)

        if r != order[-1]:
            add_columns(r, 1.0)

    d_copies = []
    for i, (k, e) in enumerate(far):
        peer, slot = far_peer(k, e)
        d_copies.append(
            remote(row_send.at[rows_of(peer)], land_far.at[slot], d_send.at[i], d_recv.at[slot], rep=peer)
        )
    p_copy = remote(row_acc.at[rows_of(partner)], land_pair, p_send, p_recv, rep=partner)
    for copy in d_copies + [p_copy]:
        copy.start()
    add_columns(order[-1], grad_scale)
    p_copy.wait_recv()
    mine = row_acc[rows_of(me_q), :] + land_pair[...]
    for i in range(len(far)):
        remote(
            row_send.at[rows_of(partner)], land_far.at[i], d_send.at[i], d_recv.at[i], rep=partner
        ).wait_recv()
        mine = mine + land_far[i].astype(jnp.float32)
    row_out[...] = mine * grad_scale

    for copy in u_copies + m_copies + v_copies + d_copies + [p_copy]:
        copy.wait_send()


def on_device(
    ratings, row_mask, tile_owner, tile_row, tile_col, tile_count, row_factors, col_factors
):
    n_strat, n_rep = lax.axis_size("strat"), lax.axis_size("rep")
    edge = ratings.shape[1]
    rows, width = row_factors.shape
    cols = col_factors.shape[0]
    meta_rows = 8
    tile_count = tile_count.reshape(1, 1)
    hbm = pl.BlockSpec(memory_space=pltpu.HBM)
    vmem = pl.BlockSpec(memory_space=pltpu.VMEM)
    dma = pltpu.SemaphoreType.DMA
    row_grad, col_grad = pl.pallas_call(
        functools.partial(kernel, n_strat, n_rep),
        out_shape=(
            pltpu.VMEM((rows, width), jnp.float32),
            pltpu.VMEM((cols, width), jnp.float32),
        ),
        in_specs=[hbm] * 8,
        out_specs=(vmem, vmem),
        scratch_shapes=[
            pltpu.SMEM(tile_row.shape, jnp.int32),
            pltpu.SMEM(tile_row.shape, jnp.int32),
            pltpu.SMEM(tile_col.shape, jnp.int32),
            pltpu.SMEM(tile_count.shape, jnp.int32),
            pltpu.VMEM(ratings.shape, ratings.dtype),
            pltpu.VMEM(row_mask.shape, jnp.int32),
            pltpu.VMEM((n_rep * rows, width), row_factors.dtype),
            pltpu.VMEM((cols, width), col_factors.dtype),
            pltpu.VMEM((n_strat - 1, CAP, edge, edge), ratings.dtype),
            pltpu.VMEM((n_strat - 1, meta_rows, edge), jnp.int32),
            pltpu.VMEM((n_strat, CAP, edge, edge), ratings.dtype),
            pltpu.VMEM((n_strat, meta_rows, edge), jnp.int32),
            pltpu.VMEM((n_rep * rows, width), jnp.float32),
            pltpu.VMEM((n_rep * rows, width), jnp.bfloat16),
            pltpu.VMEM((n_strat, CAP * edge, cols), jnp.bfloat16),
            pltpu.VMEM((n_strat, CAP * edge, width), jnp.bfloat16),
            pltpu.VMEM((rows, width), jnp.float32),
            pltpu.VMEM((n_rep - 2, rows, width), jnp.bfloat16),
            pltpu.VMEM((n_strat, CAP, edge, edge), jnp.float32),
            pltpu.VMEM((n_strat, CAP, edge, edge), jnp.float32),
            pltpu.VMEM((n_strat, CAP * edge, width), jnp.bfloat16),
            dma((4,)),
            dma((4,)),
            dma((n_rep - 1,)),
            dma((n_rep - 1,)),
            dma((n_strat - 1,)),
            dma((n_strat - 1,)),
            dma((n_strat - 1,)),
            dma((n_strat - 1,)),
            dma,
            dma,
            dma((n_rep - 2,)),
            dma((n_rep - 2,)),
            pltpu.SemaphoreType.REGULAR,
        ],
        compiler_params=pltpu.CompilerParams(
            collective_id=0, has_side_effects=True
        ),
        name="gradient_pass",
    )(tile_owner.reshape(-1), tile_row, tile_col, tile_count, ratings, row_mask, row_factors, col_factors)
    return row_grad, col_grad


def solution(mesh):
    return jax.shard_map(
        on_device,
        mesh=mesh,
        in_specs=(
            P(("strat", "rep"), None, None),
            P(("strat", "rep"), None),
            P(("strat", "rep"), None),
            P(("strat", "rep")),
            P(("strat", "rep")),
            P(("strat", "rep")),
            P(("strat", "rep"), None),
            P(("strat", "rep"), None),
        ),
        out_specs=(P(("strat", "rep"), None), P(("strat", "rep"), None)),
        check_vma=False,
    )
```

```python
import functools

import jax
import jax.numpy as jnp
from jax import lax
from jax.experimental import pallas as pl
from jax.experimental.pallas import tpu as pltpu
from jax.sharding import PartitionSpec as P

CAP = 2


grad_scale = 0.0625
MESH = pl.DeviceIdType.MESH


def remote(src, dst, send_sem, recv_sem, **where):
    return pltpu.make_async_remote_copy(
        src_ref=src,
        dst_ref=dst,
        send_sem=send_sem,
        recv_sem=recv_sem,
        device_id=where,
        device_id_type=MESH,
    )


def kernel(
    n_strat, n_rep,
    owner_in, tile_row_in, tile_col_in, count_in, ratings, row_mask, row_factors, col_factors,
    row_out, col_out,
    owner, tile_row, tile_col, count,
    tiles, masks, row_all, col_all, send_vals, send_meta, recv_vals, recv_meta,
    row_acc, row_send, col_errors, row_picks, land_pair, land_far,
    predictions, keeps, col_picks,
    small_sem, local_sem, u_send, u_recv, v_send, v_recv, m_send, m_recv,
    p_send, p_recv, d_send, d_recv, ready, strat_in, pair_in,
):
    held, edge = tiles.shape[0], tiles.shape[1]
    rows = row_factors.shape[0]
    n_row, n_col = row_all.shape[0] // edge, col_all.shape[0] // edge
    me_s, me_q = lax.axis_index("strat"), lax.axis_index("rep")
    pairs = n_rep // 2
    chip, side = me_q // 2, lax.rem(me_q, 2)
    partner = 2 * chip + 1 - side
    peers, own = n_strat - 1, n_strat - 1
    phases, half = send_vals.shape[1], send_vals.shape[3]

    def rows_of(index):
        return pl.ds(pl.multiple_of(index * rows, rows), rows)

    def other(k, me):
        past = jnp.where(k >= me, 1, 0)
        return k + past, me - 1 + past

    def pick(blocks, same):
        wide = blocks.shape[1] // edge
        chosen = None
        for b, flag in enumerate(same):
            flag = jnp.concatenate([flag] * wide, axis=1)
            weight = jnp.broadcast_to(flag, (edge, wide * edge)).astype(blocks.dtype)
            part = blocks[b * edge : (b + 1) * edge, :] * weight
            chosen = part if chosen is None else chosen + part
        return chosen

    local = [
        pltpu.make_async_copy(row_mask, masks, local_sem.at[0]),
        pltpu.make_async_copy(ratings, tiles, local_sem.at[1]),
        pltpu.make_async_copy(row_factors, row_all.at[rows_of(me_q)], local_sem.at[2]),
        pltpu.make_async_copy(col_factors, col_all, local_sem.at[3]),
    ]
    small = [
        pltpu.make_async_copy(source, target, small_sem.at[i])
        for i, (source, target) in enumerate(
            [(owner_in, owner), (tile_row_in, tile_row), (tile_col_in, tile_col), (count_in, count)]
        )
    ]
    for copy in small + local[:2]:
        copy.start()

    barrier = pltpu.get_barrier_semaphore()

    def signal(semaphore, **where):
        pl.semaphore_signal(semaphore, inc=1, device_id=where, device_id_type=MESH)

    for k in range(pairs - 1):
        @pl.when(k >= chip)
        def _():
            signal(barrier, rep=2 * k + 3)

    signal(barrier, rep=partner)
    for k in range(peers):
        @pl.when(k >= me_s)
        def _():
            signal(barrier, strat=k + 1, rep=2 * chip)

    for copy in local[2:]:
        copy.start()

    for copy in small:
        copy.wait()

    live = [p < count[0, 0] for p in range(held)]
    owners = [owner[p] for p in range(held)]
    plan = []
    for k in range(n_strat):
        dest = me_s if k == own else other(k, me_s)[0]
        seen = jnp.int32(0)
        flags = [[] for _ in range(CAP)]
        slot_ids = [[jnp.int32(0), jnp.int32(0)] for _ in range(CAP)]
        for p in range(held):
            here = jnp.where(jnp.logical_and(live[p], owners[p] == dest), 1, 0)
            for i in range(CAP):
                flag = jnp.where(seen == i, here, 0)
                flags[i].append(flag)
                slot_ids[i][0] += flag * tile_row[p]
                slot_ids[i][1] += flag * tile_col[p]
            seen = seen + here
        plan.append((flags, slot_ids))

    local[0].wait()
    for k in range(n_strat):
        flags, slot_ids = plan[k]
        meta = recv_meta.at[own] if k == own else send_meta.at[k]
        for i in range(CAP):
            row = masks[0:1, :] * flags[i][0]
            for p in range(1, held):
                row = row + masks[p : p + 1, :] * flags[i][p]
            meta[i : i + 1, :] = row
            for j in range(2):
                at = (1 + j) * CAP + i
                meta[at : at + 1, :] = jnp.full((1, edge), slot_ids[i][j], jnp.int32)
        meta[3 * CAP :, :] = jnp.zeros((meta.shape[0] - 3 * CAP, edge), jnp.int32)
    local[1].wait()
    for k in range(n_strat):
        flags, _ = plan[k]
        slots = recv_vals.at[own] if k == own else send_vals.at[k]
        for i in range(CAP):
            value = None
            for p in range(held):
                weight = jnp.full((edge, edge), flags[i][p].astype(jnp.float32)).astype(tiles.dtype)
                part = tiles[p] * weight
                value = part if value is None else value + part
            for h in range(phases):
                slots[h, i] = value[h * half : (h + 1) * half]

    m_copies, v_copies = [], []
    for k in range(peers):
        dest, slot = other(k, me_s)
        m_copies.append(
            remote(send_meta.at[k], recv_meta.at[slot], m_send.at[k], m_recv.at[slot], strat=dest)
        )
        v_copies.append(
            [
                remote(
                    send_vals.at[k, h], recv_vals.at[slot, h], v_send.at[k, h], v_recv.at[slot, h],
                    strat=dest,
                )
                for h in range(phases)
            ]
        )
    far = [(k, e) for k in range(pairs - 1) for e in range(2)]

    def far_peer(k, e):
        target, slot = other(k, chip)
        return 2 * target + lax.rem(side + e, 2), 2 * slot + e

    u_copies = []
    for i, (k, e) in enumerate(far):
        peer, slot = far_peer(k, e)
        u_copies.append(
            remote(row_factors, row_all.at[rows_of(me_q)], u_send.at[i], u_recv.at[slot], rep=peer)
        )
    u_copies.append(
        remote(
            row_factors, row_all.at[rows_of(me_q)], u_send.at[len(far)], u_recv.at[len(far)],
            rep=partner,
        )
    )

    @pl.when(side == 0)
    def _():
        pl.semaphore_wait(barrier, 2 * me_s + 1)
        signal(ready, rep=partner)
        for k in range(peers):
            @pl.when(k < me_s)
            def _():
                for e in range(2):
                    signal(strat_in.at[me_s], strat=k, rep=2 * chip + e)

    @pl.when(side == 1)
    def _():
        pl.semaphore_wait(ready, 1)

    for k in range(peers):
        @pl.when(k < me_s)
        def _():
            m_copies[k].start()
            for copy in v_copies[k]:
                copy.start()

    @pl.when(side == 1)
    def _():
        pl.semaphore_wait(barrier, 2 * chip + 1)
        signal(ready, rep=partner)
        for k in range(pairs - 1):
            @pl.when(k < chip)
            def _():
                for e in range(2):
                    signal(pair_in.at[chip], rep=2 * k + e)

    @pl.when(side == 0)
    def _():
        pl.semaphore_wait(ready, 1)

    for k in range(pairs - 1):
        @pl.when(k < chip)
        def _():
            for e in range(2):
                u_copies[2 * k + e].start()

    u_copies[-1].start()
    for k in range(pairs - 1):
        @pl.when(k >= chip)
        def _():
            pl.semaphore_wait(pair_in.at[k + 1], 1)
            for e in range(2):
                u_copies[2 * k + e].start()

    for k in range(peers):
        @pl.when(k >= me_s)
        def _():
            pl.semaphore_wait(strat_in.at[k + 1], 1)
            m_copies[k].start()
            for copy in v_copies[k]:
                copy.start()

    order = [own] + list(range(peers))

    def m_at(slot):
        return remote(
            send_meta.at[slot], recv_meta.at[slot], m_send.at[slot], m_recv.at[slot],
            strat=other(slot, me_s)[0],
        )

    def v_at(slot, h):
        return remote(
            send_vals.at[slot, h], recv_vals.at[slot, h], v_send.at[slot, h], v_recv.at[slot, h],
            strat=other(slot, me_s)[0],
        )

    def u_at(slot):
        return remote(
            row_factors, row_all.at[rows_of(me_q)], u_send.at[slot], u_recv.at[slot], rep=partner
        )

    for k in range(peers):
        m_at(k).wait_recv()
    local[2].wait()
    local[3].wait()
    for i in range(n_rep - 1):
        u_at(i).wait_recv()

    def flags_of(r):
        meta = recv_meta[r].astype(jnp.float32)
        in_row, in_col = [], []
        for k in range(CAP):
            row_id, col_id = (meta[(1 + i) * CAP + k : (1 + i) * CAP + k + 1, :] for i in range(2))
            in_row.append([jnp.where(row_id == b, 1.0, 0.0) for b in range(n_row)])
            in_col.append([jnp.where(col_id == c, 1.0, 0.0) for c in range(n_col)])
        return meta, in_row, in_col

    for r in order:
        meta, in_row, in_col = flags_of(r)
        keep = meta.T
        for k in range(CAP):
            row_pick, col_pick = pick(row_all, in_row[k]), pick(col_all, in_col[k])
            row_picks[r, k * edge : (k + 1) * edge, :] = row_pick
            col_picks[r, k * edge : (k + 1) * edge, :] = col_pick
            predictions[r, k] = lax.dot_general(
                row_pick, col_pick, (((1,), (1,)), ((), ())), preferred_element_type=jnp.float32
            )
            keeps[r, k] = jnp.broadcast_to(keep[:, k : k + 1], (edge, edge))

    def add_columns(r, scale):
        term = lax.dot_general(
            col_errors[r], row_picks[r], (((0,), (0,)), ((), ())),
            preferred_element_type=jnp.float32,
        )
        if r != order[0]:
            term = col_out[...] + term
        col_out[...] = term * scale

    d_copies = []
    p_copy = remote(row_acc.at[rows_of(partner)], land_pair, p_send, p_recv, rep=partner)
    for h in range(phases):
        for r in order:
            _, row_same, in_col = flags_of(r)
            if r != own:
                v_at(r, h).wait_recv()
            errors = []
            for k in range(CAP):
                mine = slice(h * half, (h + 1) * half)
                error = keeps[r, k, mine, :] * (
                    predictions[r, k, mine, :] - recv_vals[r, h, k].astype(jnp.float32)
                )
                errors.append(error)
                at = k * edge + h * half
                for c in range(n_col):
                    col_errors[r, at : at + half, c * edge : (c + 1) * edge] = (
                        error * in_col[k][c]
                    ).astype(jnp.bfloat16)
            stacked = col_picks[r]
            for b in range(n_row):
                left = jnp.concatenate(
                    [(errors[k] * row_same[k][b]).astype(jnp.bfloat16) for k in range(CAP)], axis=1
                )
                term = jnp.dot(left, stacked, preferred_element_type=jnp.float32)
                block = slice(b * edge + h * half, b * edge + (h + 1) * half)
                if r != order[0]:
                    term = row_acc[block, :] + term
                row_acc[block, :] = term
                if r == order[-1]:
                    row_send[block, :] = term.astype(row_send.dtype)

            if h == phases - 1 and r != order[-1]:
                add_columns(r, 1.0)

        for k in range(pairs - 1):
            for e in [lax.rem(side + h, 2)] if phases == 2 else range(2):
                peer, slot = far_peer(k, e)
                i = len(d_copies)
                copy = remote(
                    row_send.at[rows_of(peer)], land_far.at[slot], d_send.at[i], d_recv.at[slot],
                    rep=peer,
                )
                copy.start()
                d_copies.append(copy)
        if phases == 2:
            pl.when(side == 1 - h)(p_copy.start)
        else:
            p_copy.start()
    add_columns(order[-1], grad_scale)
    p_copy.wait_recv()
    mine = row_acc[rows_of(me_q), :] + land_pair[...]
    for i in range(len(far)):
        remote(
            row_send.at[rows_of(partner)], land_far.at[i], d_send.at[i], d_recv.at[i], rep=partner
        ).wait_recv()
        mine = mine + land_far[i].astype(jnp.float32)
    row_out[...] = mine * grad_scale

    for copy in u_copies + m_copies + sum(v_copies, []) + d_copies + [p_copy]:
        copy.wait_send()


def on_device(
    ratings, row_mask, tile_owner, tile_row, tile_col, tile_count, row_factors, col_factors
):
    n_strat, n_rep = lax.axis_size("strat"), lax.axis_size("rep")
    edge = ratings.shape[1]
    rows, width = row_factors.shape
    cols = col_factors.shape[0]
    meta_rows = 8
    phases = 2 if edge == 2 * rows else 1
    tile_count = tile_count.reshape(1, 1)
    hbm = pl.BlockSpec(memory_space=pltpu.HBM)
    vmem = pl.BlockSpec(memory_space=pltpu.VMEM)
    dma = pltpu.SemaphoreType.DMA
    row_grad, col_grad = pl.pallas_call(
        functools.partial(kernel, n_strat, n_rep),
        out_shape=(
            pltpu.VMEM((rows, width), jnp.float32),
            pltpu.VMEM((cols, width), jnp.float32),
        ),
        in_specs=[hbm] * 8,
        out_specs=(vmem, vmem),
        scratch_shapes=[
            pltpu.SMEM(tile_row.shape, jnp.int32),
            pltpu.SMEM(tile_row.shape, jnp.int32),
            pltpu.SMEM(tile_col.shape, jnp.int32),
            pltpu.SMEM(tile_count.shape, jnp.int32),
            pltpu.VMEM(ratings.shape, ratings.dtype),
            pltpu.VMEM(row_mask.shape, jnp.int32),
            pltpu.VMEM((n_rep * rows, width), row_factors.dtype),
            pltpu.VMEM((cols, width), col_factors.dtype),
            pltpu.VMEM((n_strat - 1, phases, CAP, edge // phases, edge), ratings.dtype),
            pltpu.VMEM((n_strat - 1, meta_rows, edge), jnp.int32),
            pltpu.VMEM((n_strat, phases, CAP, edge // phases, edge), ratings.dtype),
            pltpu.VMEM((n_strat, meta_rows, edge), jnp.int32),
            pltpu.VMEM((n_rep * rows, width), jnp.float32),
            pltpu.VMEM((n_rep * rows, width), jnp.bfloat16),
            pltpu.VMEM((n_strat, CAP * edge, cols), jnp.bfloat16),
            pltpu.VMEM((n_strat, CAP * edge, width), jnp.bfloat16),
            pltpu.VMEM((rows, width), jnp.float32),
            pltpu.VMEM((n_rep - 2, rows, width), jnp.bfloat16),
            pltpu.VMEM((n_strat, CAP, edge, edge), jnp.float32),
            pltpu.VMEM((n_strat, CAP, edge, edge), jnp.float32),
            pltpu.VMEM((n_strat, CAP * edge, width), jnp.bfloat16),
            dma((4,)),
            dma((4,)),
            dma((n_rep - 1,)),
            dma((n_rep - 1,)),
            dma((n_strat - 1, phases)),
            dma((n_strat - 1, phases)),
            dma((n_strat - 1,)),
            dma((n_strat - 1,)),
            dma,
            dma,
            dma((n_rep - 2,)),
            dma((n_rep - 2,)),
            pltpu.SemaphoreType.REGULAR,
            pltpu.SemaphoreType.REGULAR((n_strat,)),
            pltpu.SemaphoreType.REGULAR((n_rep // 2,)),
        ],
        compiler_params=pltpu.CompilerParams(
            collective_id=0, has_side_effects=True
        ),
        name="gradient_pass",
    )(tile_owner.reshape(-1), tile_row, tile_col, tile_count, ratings, row_mask, row_factors, col_factors)
    return row_grad, col_grad


def solution(mesh):
    return jax.shard_map(
        on_device,
        mesh=mesh,
        in_specs=(
            P(("strat", "rep"), None, None),
            P(("strat", "rep"), None),
            P(("strat", "rep"), None),
            P(("strat", "rep")),
            P(("strat", "rep")),
            P(("strat", "rep")),
            P(("strat", "rep"), None),
            P(("strat", "rep"), None),
        ),
        out_specs=(P(("strat", "rep"), None), P(("strat", "rep"), None)),
        check_vma=False,
    )
```

```python
import functools

import jax
import jax.numpy as jnp
from jax import lax
from jax.experimental import pallas as pl
from jax.experimental.pallas import tpu as pltpu
from jax.sharding import PartitionSpec as P

CAP = 2
TURNS = 1


grad_scale = 0.0625
MESH = pl.DeviceIdType.MESH


def remote(src, dst, send_sem, recv_sem, **where):
    return pltpu.make_async_remote_copy(
        src_ref=src,
        dst_ref=dst,
        send_sem=send_sem,
        recv_sem=recv_sem,
        device_id=where,
        device_id_type=MESH,
    )


def kernel(
    n_strat, n_rep,
    owner_in, tile_row_in, tile_col_in, count_in, ratings, row_mask, row_factors, col_factors,
    row_out, col_out,
    owner, tile_row, tile_col, count,
    tiles, masks, row_all, col_all, send_vals, send_meta, recv_vals, recv_meta,
    row_acc, row_send, col_errors, row_picks, land_pair, land_far,
    predictions, keeps, col_picks,
    small_sem, local_sem, u_send, u_recv, v_send, v_recv, m_send, m_recv,
    p_send, p_recv, d_send, d_recv, ready, strat_in, pair_in,
):
    held, edge = tiles.shape[0], tiles.shape[1]
    rows = row_factors.shape[0]
    n_row, n_col = row_all.shape[0] // edge, col_all.shape[0] // edge
    me_s, me_q = lax.axis_index("strat"), lax.axis_index("rep")
    pairs = n_rep // 2
    chip, side = me_q // 2, lax.rem(me_q, 2)
    partner = 2 * chip + 1 - side
    peers, own = n_strat - 1, n_strat - 1
    phases, part = send_vals.shape[1], send_vals.shape[3]
    turns = max(1, phases // 2)
    piece = rows // turns

    def rows_of(index):
        return pl.ds(pl.multiple_of(index * rows, rows), rows)

    def first_row(h):
        return h % 2 * rows + h // 2 * part if phases > 1 else 0

    def other(k, me):
        past = jnp.where(k >= me, 1, 0)
        return k + past, me - 1 + past

    def pick(blocks, same):
        wide = blocks.shape[1] // edge
        chosen = None
        for b, flag in enumerate(same):
            flag = jnp.concatenate([flag] * wide, axis=1)
            weight = jnp.broadcast_to(flag, (edge, wide * edge)).astype(blocks.dtype)
            part = blocks[b * edge : (b + 1) * edge, :] * weight
            chosen = part if chosen is None else chosen + part
        return chosen

    local = [
        pltpu.make_async_copy(row_mask, masks, local_sem.at[0]),
        pltpu.make_async_copy(ratings, tiles, local_sem.at[1]),
        pltpu.make_async_copy(row_factors, row_all.at[rows_of(me_q)], local_sem.at[2]),
        pltpu.make_async_copy(col_factors, col_all, local_sem.at[3]),
    ]
    small = [
        pltpu.make_async_copy(source, target, small_sem.at[i])
        for i, (source, target) in enumerate(
            [(owner_in, owner), (tile_row_in, tile_row), (tile_col_in, tile_col), (count_in, count)]
        )
    ]
    for copy in small + local[:2]:
        copy.start()

    barrier = pltpu.get_barrier_semaphore()

    def signal(semaphore, **where):
        pl.semaphore_signal(semaphore, inc=1, device_id=where, device_id_type=MESH)

    for k in range(pairs - 1):
        @pl.when(k >= chip)
        def _():
            signal(barrier, rep=2 * k + 3)

    signal(barrier, rep=partner)
    for k in range(peers):
        @pl.when(k >= me_s)
        def _():
            signal(barrier, strat=k + 1, rep=2 * chip)

    for copy in local[2:]:
        copy.start()

    @pl.when(side == 0)
    def _():
        pl.semaphore_wait(barrier, 2 * me_s + 1)
        signal(ready, rep=partner)
        for k in range(peers):
            @pl.when(k < me_s)
            def _():
                for e in range(2):
                    signal(strat_in.at[me_s], strat=k, rep=2 * chip + e)

    for copy in small:
        copy.wait()

    live = [p < count[0, 0] for p in range(held)]
    owners = [owner[p] for p in range(held)]
    plan = []
    for k in range(n_strat):
        dest = me_s if k == own else other(k, me_s)[0]
        seen = jnp.int32(0)
        flags = [[] for _ in range(CAP)]
        slot_ids = [[jnp.int32(0), jnp.int32(0)] for _ in range(CAP)]
        for p in range(held):
            here = jnp.where(jnp.logical_and(live[p], owners[p] == dest), 1, 0)
            for i in range(CAP):
                flag = jnp.where(seen == i, here, 0)
                flags[i].append(flag)
                slot_ids[i][0] += flag * tile_row[p]
                slot_ids[i][1] += flag * tile_col[p]
            seen = seen + here
        plan.append((flags, slot_ids))

    local[0].wait()
    for k in range(n_strat):
        flags, slot_ids = plan[k]
        meta = recv_meta.at[own] if k == own else send_meta.at[k]
        for i in range(CAP):
            row = masks[0:1, :] * flags[i][0]
            for p in range(1, held):
                row = row + masks[p : p + 1, :] * flags[i][p]
            meta[i : i + 1, :] = row
            for j in range(2):
                at = (1 + j) * CAP + i
                meta[at : at + 1, :] = jnp.full((1, edge), slot_ids[i][j], jnp.int32)
        meta[3 * CAP :, :] = jnp.zeros((meta.shape[0] - 3 * CAP, edge), jnp.int32)
    local[1].wait()
    for k in range(n_strat):
        flags, _ = plan[k]
        slots = recv_vals.at[own] if k == own else send_vals.at[k]
        for i in range(CAP):
            value = None
            for p in range(held):
                weight = jnp.full((edge, edge), flags[i][p].astype(jnp.float32)).astype(tiles.dtype)
                term = tiles[p] * weight
                value = term if value is None else value + term
            for h in range(phases):
                slots[h, i] = value[first_row(h) : first_row(h) + part]

    m_copies, v_copies = [], []
    for k in range(peers):
        dest, slot = other(k, me_s)
        m_copies.append(
            remote(send_meta.at[k], recv_meta.at[slot], m_send.at[k], m_recv.at[slot], strat=dest)
        )
        v_copies.append(
            [
                remote(
                    send_vals.at[k, h], recv_vals.at[slot, h], v_send.at[k, h], v_recv.at[slot, h],
                    strat=dest,
                )
                for h in range(phases)
            ]
        )
    far = [(k, e) for k in range(pairs - 1) for e in range(2)]

    def far_peer(k, e):
        target, slot = other(k, chip)
        return 2 * target + lax.rem(side + e, 2), 2 * slot + e

    u_copies = []
    for i, (k, e) in enumerate(far):
        peer, slot = far_peer(k, e)
        u_copies.append(
            remote(row_factors, row_all.at[rows_of(me_q)], u_send.at[i], u_recv.at[slot], rep=peer)
        )
    u_copies.append(
        remote(
            row_factors, row_all.at[rows_of(me_q)], u_send.at[len(far)], u_recv.at[len(far)],
            rep=partner,
        )
    )

    @pl.when(side == 1)
    def _():
        pl.semaphore_wait(ready, 1)

    @pl.when(me_s > 0)
    def _():
        m_copies[0].start()
        for copy in v_copies[0]:
            copy.start()

    @pl.when(side == 1)
    def _():
        pl.semaphore_wait(barrier, 2 * chip + 1)
        signal(ready, rep=partner)
        for k in range(pairs - 1):
            @pl.when(k < chip)
            def _():
                for e in range(2):
                    signal(pair_in.at[chip], rep=2 * k + e)

    @pl.when(side == 0)
    def _():
        pl.semaphore_wait(ready, 1)

    for k in range(pairs - 1):
        @pl.when(k < chip)
        def _():
            for e in range(2):
                u_copies[2 * k + e].start()

    u_copies[-1].start()
    for k in range(pairs - 1):
        @pl.when(k >= chip)
        def _():
            pl.semaphore_wait(pair_in.at[k + 1], 1)
            for e in range(2):
                u_copies[2 * k + e].start()

    for k in list(range(1, peers))[::-1]:
        @pl.when(k < me_s)
        def _():
            m_copies[k].start()
            for copy in v_copies[k]:
                copy.start()

    for k in range(peers):
        @pl.when(k >= me_s)
        def _():
            pl.semaphore_wait(strat_in.at[k + 1], 1)
            m_copies[k].start()
            for copy in v_copies[k]:
                copy.start()

    order = [own] + list(range(peers))

    def m_at(slot):
        return remote(
            send_meta.at[slot], recv_meta.at[slot], m_send.at[slot], m_recv.at[slot],
            strat=other(slot, me_s)[0],
        )

    def v_at(slot, h):
        return remote(
            send_vals.at[slot, h], recv_vals.at[slot, h], v_send.at[slot, h], v_recv.at[slot, h],
            strat=other(slot, me_s)[0],
        )

    def u_at(slot):
        return remote(
            row_factors, row_all.at[rows_of(me_q)], u_send.at[slot], u_recv.at[slot], rep=partner
        )

    for k in range(peers):
        m_at(k).wait_recv()
    local[2].wait()
    local[3].wait()
    for i in range(n_rep - 1):
        u_at(i).wait_recv()

    def flags_of(r):
        meta = recv_meta[r].astype(jnp.float32)
        in_row, in_col = [], []
        for k in range(CAP):
            row_id, col_id = (meta[(1 + i) * CAP + k : (1 + i) * CAP + k + 1, :] for i in range(2))
            in_row.append([jnp.where(row_id == b, 1.0, 0.0) for b in range(n_row)])
            in_col.append([jnp.where(col_id == c, 1.0, 0.0) for c in range(n_col)])
        return meta, in_row, in_col

    for r in order:
        meta, in_row, in_col = flags_of(r)
        keep = meta.T
        for k in range(CAP):
            row_pick, col_pick = pick(row_all, in_row[k]), pick(col_all, in_col[k])
            row_picks[r, k * edge : (k + 1) * edge, :] = row_pick
            col_picks[r, k * edge : (k + 1) * edge, :] = col_pick
            predictions[r, k] = lax.dot_general(
                row_pick, col_pick, (((1,), (1,)), ((), ())), preferred_element_type=jnp.float32
            )
            keeps[r, k] = jnp.broadcast_to(keep[:, k : k + 1], (edge, edge))

    def add_columns(r, scale):
        term = lax.dot_general(
            col_errors[r], row_picks[r], (((0,), (0,)), ((), ())),
            preferred_element_type=jnp.float32,
        )
        if r != order[0]:
            term = col_out[...] + term
        col_out[...] = term * scale

    d_copies, p_copies = [], []
    for h in range(phases):
        for r in order:
            _, row_same, in_col = flags_of(r)
            if r != own:
                v_at(r, h).wait_recv()
            errors = []
            for k in range(CAP):
                here = slice(first_row(h), first_row(h) + part)
                error = keeps[r, k, here, :] * (
                    predictions[r, k, here, :] - recv_vals[r, h, k].astype(jnp.float32)
                )
                errors.append(error)
                at = k * edge + first_row(h)
                for c in range(n_col):
                    col_errors[r, at : at + part, c * edge : (c + 1) * edge] = (
                        error * in_col[k][c]
                    ).astype(jnp.bfloat16)
            left = jnp.concatenate(
                [
                    jnp.concatenate(
                        [(errors[k] * row_same[k][b]).astype(jnp.bfloat16) for k in range(CAP)], axis=1
                    )
                    for b in range(n_row)
                ],
                axis=0,
            )
            term = jnp.dot(left, col_picks[r], preferred_element_type=jnp.float32)
            if r != order[0]:
                term = row_acc[h] + term
            row_acc[h] = term
            if r == order[-1]:
                row_send[h] = term.astype(row_send.dtype)

            if h == phases - 1 and r != order[-1]:
                add_columns(r, 1.0)

        turn = h // 2
        within = pl.ds(turn * piece, piece)
        for k in range(pairs - 1):
            for e in [lax.rem(side + h, 2)] if phases > 1 else range(2):
                peer, slot = far_peer(k, e)
                start = peer // 2 * piece if phases > 1 else peer * piece
                i = len(d_copies)
                copy = remote(
                    row_send.at[h, pl.ds(pl.multiple_of(start, piece), piece)],
                    land_far.at[slot, within], d_send.at[i], d_recv.at[slot, turn], rep=peer,
                )
                copy.start()
                d_copies.append(copy)
        if phases == 1 or h % 2:
            start = chip * piece if phases > 1 else partner * piece
            which = 2 * turn + 1 - side if phases > 1 else 0
            p_copies.append(
                remote(
                    row_acc.at[which, pl.ds(pl.multiple_of(start, piece), piece)],
                    land_pair.at[within], p_send.at[turn], p_recv.at[turn], rep=partner,
                )
            )
        if phases == 1:
            p_copies[turn].start()
        elif h % 2:
            pl.when(side == 0)(p_copies[turn].start)
        else:
            pl.when(side == 1)(
                remote(
                    row_acc.at[h, pl.ds(pl.multiple_of(chip * piece, piece), piece)],
                    land_pair.at[within], p_send.at[turn], p_recv.at[turn], rep=partner,
                ).start
            )
    add_columns(order[-1], grad_scale)
    for turn in range(turns):
        within = pl.ds(turn * piece, piece)
        p_copies[turn].wait_recv()
        which, start = (2 * turn + side, chip * piece) if phases > 1 else (0, me_q * piece)
        mine = row_acc[which, pl.ds(pl.multiple_of(start, piece), piece), :] + land_pair[within, :]
        for i in range(len(far)):
            remote(
                row_send.at[0, pl.ds(0, piece)], land_far.at[i, within], d_send.at[i],
                d_recv.at[i, turn], rep=partner,
            ).wait_recv()
            mine = mine + land_far[i, within, :].astype(jnp.float32)
        row_out[within, :] = mine * grad_scale

    for copy in u_copies + m_copies + sum(v_copies, []) + d_copies + p_copies:
        copy.wait_send()


def on_device(
    ratings, row_mask, tile_owner, tile_row, tile_col, tile_count, row_factors, col_factors
):
    n_strat, n_rep = lax.axis_size("strat"), lax.axis_size("rep")
    edge = ratings.shape[1]
    rows, width = row_factors.shape
    cols = col_factors.shape[0]
    meta_rows = 8
    phases = 1
    if edge == 2 * rows and rows % (16 * TURNS) == 0:
        phases = 2 * TURNS
    turns = max(1, phases // 2)
    tile_count = tile_count.reshape(1, 1)
    hbm = pl.BlockSpec(memory_space=pltpu.HBM)
    vmem = pl.BlockSpec(memory_space=pltpu.VMEM)
    dma = pltpu.SemaphoreType.DMA
    row_grad, col_grad = pl.pallas_call(
        functools.partial(kernel, n_strat, n_rep),
        out_shape=(
            pltpu.VMEM((rows, width), jnp.float32),
            pltpu.VMEM((cols, width), jnp.float32),
        ),
        in_specs=[hbm] * 8,
        out_specs=(vmem, vmem),
        scratch_shapes=[
            pltpu.SMEM(tile_row.shape, jnp.int32),
            pltpu.SMEM(tile_row.shape, jnp.int32),
            pltpu.SMEM(tile_col.shape, jnp.int32),
            pltpu.SMEM(tile_count.shape, jnp.int32),
            pltpu.VMEM(ratings.shape, ratings.dtype),
            pltpu.VMEM(row_mask.shape, jnp.int32),
            pltpu.VMEM((n_rep * rows, width), row_factors.dtype),
            pltpu.VMEM((cols, width), col_factors.dtype),
            pltpu.VMEM((n_strat - 1, phases, CAP, edge // phases, edge), ratings.dtype),
            pltpu.VMEM((n_strat - 1, meta_rows, edge), jnp.int32),
            pltpu.VMEM((n_strat, phases, CAP, edge // phases, edge), ratings.dtype),
            pltpu.VMEM((n_strat, meta_rows, edge), jnp.int32),
            pltpu.VMEM((phases, n_rep * rows // phases, width), jnp.float32),
            pltpu.VMEM((phases, n_rep * rows // phases, width), jnp.bfloat16),
            pltpu.VMEM((n_strat, CAP * edge, cols), jnp.bfloat16),
            pltpu.VMEM((n_strat, CAP * edge, width), jnp.bfloat16),
            pltpu.VMEM((rows, width), jnp.float32),
            pltpu.VMEM((n_rep - 2, rows, width), jnp.bfloat16),
            pltpu.VMEM((n_strat, CAP, edge, edge), jnp.float32),
            pltpu.VMEM((n_strat, CAP, edge, edge), jnp.float32),
            pltpu.VMEM((n_strat, CAP * edge, width), jnp.bfloat16),
            dma((4,)),
            dma((4,)),
            dma((n_rep - 1,)),
            dma((n_rep - 1,)),
            dma((n_strat - 1, phases)),
            dma((n_strat - 1, phases)),
            dma((n_strat - 1,)),
            dma((n_strat - 1,)),
            dma((turns,)),
            dma((turns,)),
            dma((turns * (n_rep - 2),)),
            dma((n_rep - 2, turns)),
            pltpu.SemaphoreType.REGULAR,
            pltpu.SemaphoreType.REGULAR((n_strat,)),
            pltpu.SemaphoreType.REGULAR((n_rep // 2,)),
        ],
        compiler_params=pltpu.CompilerParams(
            collective_id=0, has_side_effects=True
        ),
        name="gradient_pass",
    )(tile_owner.reshape(-1), tile_row, tile_col, tile_count, ratings, row_mask, row_factors, col_factors)
    return row_grad, col_grad


def solution(mesh):
    return jax.shard_map(
        on_device,
        mesh=mesh,
        in_specs=(
            P(("strat", "rep"), None, None),
            P(("strat", "rep"), None),
            P(("strat", "rep"), None),
            P(("strat", "rep")),
            P(("strat", "rep")),
            P(("strat", "rep")),
            P(("strat", "rep"), None),
            P(("strat", "rep"), None),
        ),
        out_specs=(P(("strat", "rep"), None), P(("strat", "rep"), None)),
        check_vma=False,
    )
```

```python
import functools

import jax
import jax.numpy as jnp
from jax import lax
from jax.experimental import pallas as pl
from jax.experimental.pallas import tpu as pltpu
from jax.sharding import PartitionSpec as P

CAP = 2
TURNS = 1


grad_scale = 0.0625
MESH = pl.DeviceIdType.MESH


def remote(src, dst, send_sem, recv_sem, **where):
    return pltpu.make_async_remote_copy(
        src_ref=src,
        dst_ref=dst,
        send_sem=send_sem,
        recv_sem=recv_sem,
        device_id=where,
        device_id_type=MESH,
    )


def kernel(
    n_strat, n_rep,
    owner_in, tile_row_in, tile_col_in, count_in, ratings, row_mask, row_factors, col_factors,
    row_out, col_out,
    owner, tile_row, tile_col, count,
    tiles, masks, row_all, col_all, send_vals, send_meta, recv_vals, recv_meta,
    row_acc, row_send, col_errors, row_picks, land_pair, land_far,
    predictions, keeps, col_picks,
    small_sem, local_sem, u_send, u_recv, v_send, v_recv, m_send, m_recv,
    p_send, p_recv, d_send, d_recv, ready, strat_in, pair_in,
):
    held, edge = tiles.shape[0], tiles.shape[1]
    rows = row_factors.shape[0]
    n_row, n_col = row_all.shape[0] // edge, col_all.shape[0] // edge
    me_s, me_q = lax.axis_index("strat"), lax.axis_index("rep")
    pairs = n_rep // 2
    chip, side = me_q // 2, lax.rem(me_q, 2)
    partner = 2 * chip + 1 - side
    peers, own = n_strat - 1, n_strat - 1
    phases, part = send_vals.shape[1], send_vals.shape[3]
    turns = max(1, phases // 2)
    piece = rows // turns

    def rows_of(index):
        return pl.ds(pl.multiple_of(index * rows, rows), rows)

    def first_row(h):
        return h % 2 * rows + h // 2 * part if phases > 1 else 0

    def other(k, me):
        past = jnp.where(k >= me, 1, 0)
        return k + past, me - 1 + past

    def pick(blocks, same):
        wide = blocks.shape[1] // edge
        chosen = None
        for b, flag in enumerate(same):
            flag = jnp.concatenate([flag] * wide, axis=1)
            weight = jnp.broadcast_to(flag, (edge, wide * edge)).astype(blocks.dtype)
            part = blocks[b * edge : (b + 1) * edge, :] * weight
            chosen = part if chosen is None else chosen + part
        return chosen

    local = [
        pltpu.make_async_copy(row_mask, masks, local_sem.at[0]),
        pltpu.make_async_copy(ratings, tiles, local_sem.at[1]),
        pltpu.make_async_copy(row_factors, row_all.at[rows_of(me_q)], local_sem.at[2]),
        pltpu.make_async_copy(col_factors, col_all, local_sem.at[3]),
    ]
    small = [
        pltpu.make_async_copy(source, target, small_sem.at[i])
        for i, (source, target) in enumerate(
            [(owner_in, owner), (tile_row_in, tile_row), (tile_col_in, tile_col), (count_in, count)]
        )
    ]
    for copy in small + local[:2]:
        copy.start()

    barrier = pltpu.get_barrier_semaphore()

    def signal(semaphore, **where):
        pl.semaphore_signal(semaphore, inc=1, device_id=where, device_id_type=MESH)

    for k in range(pairs - 1):
        @pl.when(k >= chip)
        def _():
            signal(barrier, rep=2 * k + 3)

    signal(barrier, rep=partner)
    for k in range(peers):
        @pl.when(k >= me_s)
        def _():
            signal(barrier, strat=k + 1, rep=2 * chip)

    for copy in local[2:]:
        copy.start()

    @pl.when(side == 0)
    def _():
        pl.semaphore_wait(barrier, 2 * me_s + 1)
        signal(ready, rep=partner)
        for k in range(peers):
            @pl.when(k < me_s)
            def _():
                for e in range(2):
                    signal(strat_in.at[me_s], strat=k, rep=2 * chip + e)

    for copy in small:
        copy.wait()

    live = [p < count[0, 0] for p in range(held)]
    owners = [owner[p] for p in range(held)]
    plan = []
    for k in range(n_strat):
        dest = me_s if k == own else other(k, me_s)[0]
        seen = jnp.int32(0)
        flags = [[] for _ in range(CAP)]
        slot_ids = [[jnp.int32(0), jnp.int32(0)] for _ in range(CAP)]
        for p in range(held):
            here = jnp.where(jnp.logical_and(live[p], owners[p] == dest), 1, 0)
            for i in range(CAP):
                flag = jnp.where(seen == i, here, 0)
                flags[i].append(flag)
                slot_ids[i][0] += flag * tile_row[p]
                slot_ids[i][1] += flag * tile_col[p]
            seen = seen + here
        plan.append((flags, slot_ids))

    local[0].wait()
    for k in range(n_strat):
        flags, slot_ids = plan[k]
        meta = recv_meta.at[own] if k == own else send_meta.at[k]
        for i in range(CAP):
            row = masks[0:1, :] * flags[i][0]
            for p in range(1, held):
                row = row + masks[p : p + 1, :] * flags[i][p]
            meta[i : i + 1, :] = row
            for j in range(2):
                at = (1 + j) * CAP + i
                meta[at : at + 1, :] = jnp.full((1, edge), slot_ids[i][j], jnp.int32)
        meta[3 * CAP :, :] = jnp.zeros((meta.shape[0] - 3 * CAP, edge), jnp.int32)
    local[1].wait()
    for k in range(n_strat):
        flags, _ = plan[k]
        slots = recv_vals.at[own] if k == own else send_vals.at[k]
        for i in range(CAP):
            value = None
            for p in range(held):
                weight = jnp.full((edge, edge), flags[i][p].astype(jnp.float32)).astype(tiles.dtype)
                term = tiles[p] * weight
                value = term if value is None else value + term
            for h in range(phases):
                slots[h, i] = value[first_row(h) : first_row(h) + part]

    m_copies, v_copies = [], []
    for k in range(peers):
        dest, slot = other(k, me_s)
        m_copies.append(
            remote(send_meta.at[k], recv_meta.at[slot], m_send.at[k], m_recv.at[slot], strat=dest)
        )
        v_copies.append(
            [
                remote(
                    send_vals.at[k, h], recv_vals.at[slot, h], v_send.at[k, h], v_recv.at[slot, h],
                    strat=dest,
                )
                for h in range(phases)
            ]
        )
    far = [(k, e) for k in range(pairs - 1) for e in range(2)]

    def far_peer(k, e):
        target, slot = other(k, chip)
        return 2 * target + lax.rem(side + e, 2), 2 * slot + e

    u_copies = []
    for i, (k, e) in enumerate(far):
        peer, slot = far_peer(k, e)
        u_copies.append(
            remote(row_factors, row_all.at[rows_of(me_q)], u_send.at[i], u_recv.at[slot], rep=peer)
        )
    u_copies.append(
        remote(
            row_factors, row_all.at[rows_of(me_q)], u_send.at[len(far)], u_recv.at[len(far)],
            rep=partner,
        )
    )

    @pl.when(side == 1)
    def _():
        pl.semaphore_wait(ready, 1)

    @pl.when(me_s > 0)
    def _():
        m_copies[0].start()
        for copy in v_copies[0]:
            copy.start()

    @pl.when(side == 1)
    def _():
        pl.semaphore_wait(barrier, 2 * chip + 1)
        signal(ready, rep=partner)
        for k in range(pairs - 1):
            @pl.when(k < chip)
            def _():
                for e in range(2):
                    signal(pair_in.at[chip], rep=2 * k + e)

    @pl.when(side == 0)
    def _():
        pl.semaphore_wait(ready, 1)

    for k in range(pairs - 1):
        @pl.when(k < chip)
        def _():
            for e in range(2):
                u_copies[2 * k + e].start()

    u_copies[-1].start()
    for k in range(pairs - 1):
        @pl.when(k >= chip)
        def _():
            pl.semaphore_wait(pair_in.at[k + 1], 1)
            for e in range(2):
                u_copies[2 * k + e].start()

    for k in list(range(1, peers))[::-1]:
        @pl.when(k < me_s)
        def _():
            m_copies[k].start()
            for copy in v_copies[k]:
                copy.start()

    for k in range(peers):
        @pl.when(k >= me_s)
        def _():
            pl.semaphore_wait(strat_in.at[k + 1], 1)
            m_copies[k].start()
            for copy in v_copies[k]:
                copy.start()

    order = [own] + list(range(peers))

    def m_at(slot):
        return remote(
            send_meta.at[slot], recv_meta.at[slot], m_send.at[slot], m_recv.at[slot],
            strat=other(slot, me_s)[0],
        )

    def v_at(slot, h):
        return remote(
            send_vals.at[slot, h], recv_vals.at[slot, h], v_send.at[slot, h], v_recv.at[slot, h],
            strat=other(slot, me_s)[0],
        )

    def u_at(slot):
        return remote(
            row_factors, row_all.at[rows_of(me_q)], u_send.at[slot], u_recv.at[slot], rep=partner
        )

    for k in range(peers):
        m_at(k).wait_recv()
    local[2].wait()
    local[3].wait()
    for i in range(n_rep - 1):
        u_at(i).wait_recv()

    def flags_of(r):
        meta = recv_meta[r].astype(jnp.float32)
        in_row, in_col = [], []
        for k in range(CAP):
            row_id, col_id = (meta[(1 + i) * CAP + k : (1 + i) * CAP + k + 1, :] for i in range(2))
            in_row.append([jnp.where(row_id == b, 1.0, 0.0) for b in range(n_row)])
            in_col.append([jnp.where(col_id == c, 1.0, 0.0) for c in range(n_col)])
        return meta, in_row, in_col

    for r in order:
        meta, in_row, in_col = flags_of(r)
        keep = meta.T
        for k in range(CAP):
            row_pick, col_pick = pick(row_all, in_row[k]), pick(col_all, in_col[k])
            row_picks[r, k * edge : (k + 1) * edge, :] = row_pick
            col_picks[r, k * edge : (k + 1) * edge, :] = col_pick
            predictions[r, k] = lax.dot_general(
                row_pick, col_pick, (((1,), (1,)), ((), ())), preferred_element_type=jnp.float32
            )
            keeps[r, k] = jnp.broadcast_to(keep[:, k : k + 1], (edge, edge))

    def add_columns(r, scale):
        term = lax.dot_general(
            col_errors[r], row_picks[r], (((0,), (0,)), ((), ())),
            preferred_element_type=jnp.float32,
        )
        if r != order[0]:
            term = col_out[...] + term
        col_out[...] = term * scale

    d_copies, p_copies = [], []
    for h in range(phases):
        for r in order:
            _, row_same, in_col = flags_of(r)
            if r != own:
                v_at(r, h).wait_recv()
            errors = []
            for k in range(CAP):
                here = slice(first_row(h), first_row(h) + part)
                error = keeps[r, k, here, :] * (
                    predictions[r, k, here, :] - recv_vals[r, h, k].astype(jnp.float32)
                )
                errors.append(error)
                at = k * edge + first_row(h)
                for c in range(n_col):
                    col_errors[r, at : at + part, c * edge : (c + 1) * edge] = (
                        error * in_col[k][c]
                    ).astype(jnp.bfloat16)
            left = jnp.concatenate(
                [
                    jnp.concatenate(
                        [(errors[k] * row_same[k][b]).astype(jnp.bfloat16) for k in range(CAP)], axis=1
                    )
                    for b in range(n_row)
                ],
                axis=0,
            )
            term = jnp.dot(left, col_picks[r], preferred_element_type=jnp.float32)
            if r != order[0]:
                term = row_acc[h] + term
            row_acc[h] = term
            if r == order[-1]:
                row_send[h] = term.astype(row_send.dtype)

            if h == phases - 1 and r != order[-1]:
                add_columns(r, 1.0)

        turn = h // 2
        within = pl.ds(turn * piece, piece)
        for k in range(pairs - 1):
            for e in [lax.rem(side + h, 2)] if phases > 1 else range(2):
                peer, slot = far_peer(k, e)
                start = peer // 2 * piece if phases > 1 else peer * piece
                i = len(d_copies)
                copy = remote(
                    row_send.at[h, pl.ds(pl.multiple_of(start, piece), piece)],
                    land_far.at[slot, within], d_send.at[i], d_recv.at[slot, turn], rep=peer,
                )
                copy.start()
                d_copies.append(copy)
        if phases == 1 or h % 2:
            start = chip * piece if phases > 1 else partner * piece
            which = 2 * turn + 1 - side if phases > 1 else 0
            p_copies.append(
                remote(
                    row_acc.at[which, pl.ds(pl.multiple_of(start, piece), piece)],
                    land_pair.at[within], p_send.at[turn], p_recv.at[turn], rep=partner,
                )
            )
        if phases == 1:
            p_copies[turn].start()
        elif h % 2:
            pl.when(side == 0)(p_copies[turn].start)
        else:
            pl.when(side == 1)(
                remote(
                    row_acc.at[h, pl.ds(pl.multiple_of(chip * piece, piece), piece)],
                    land_pair.at[within], p_send.at[turn], p_recv.at[turn], rep=partner,
                ).start
            )
    add_columns(order[-1], grad_scale)
    for turn in range(turns):
        within = pl.ds(turn * piece, piece)
        p_copies[turn].wait_recv()
        which, start = (2 * turn + side, chip * piece) if phases > 1 else (0, me_q * piece)
        mine = row_acc[which, pl.ds(pl.multiple_of(start, piece), piece), :] + land_pair[within, :]
        for i in range(len(far)):
            remote(
                row_send.at[0, pl.ds(0, piece)], land_far.at[i, within], d_send.at[i],
                d_recv.at[i, turn], rep=partner,
            ).wait_recv()
            mine = mine + land_far[i, within, :].astype(jnp.float32)
        row_out[within, :] = mine * grad_scale

    for copy in u_copies + m_copies + sum(v_copies, []) + d_copies + p_copies:
        copy.wait_send()


def finish(row_in, col_in, row_out, col_out, sems):
    copies = [
        pltpu.make_async_copy(col_in, col_out, sems.at[0]),
        pltpu.make_async_copy(row_in, row_out, sems.at[1]),
    ]
    for copy in copies:
        copy.start()
    for copy in copies:
        copy.wait()


def on_device(
    ratings, row_mask, tile_owner, tile_row, tile_col, tile_count, row_factors, col_factors
):
    n_strat, n_rep = lax.axis_size("strat"), lax.axis_size("rep")
    edge = ratings.shape[1]
    rows, width = row_factors.shape
    cols = col_factors.shape[0]
    meta_rows = 8
    phases = 1
    if edge == 2 * rows and rows % (16 * TURNS) == 0:
        phases = 2 * TURNS
    turns = max(1, phases // 2)
    tile_count = tile_count.reshape(1, 1)
    hbm = pl.BlockSpec(memory_space=pltpu.HBM)
    vmem = pl.BlockSpec(memory_space=pltpu.VMEM)
    dma = pltpu.SemaphoreType.DMA
    row_grad, col_grad = pl.pallas_call(
        functools.partial(kernel, n_strat, n_rep),
        out_shape=(
            pltpu.VMEM((rows, width), jnp.float32),
            pltpu.VMEM((cols, width), jnp.float32),
        ),
        in_specs=[hbm] * 8,
        out_specs=(vmem, vmem),
        scratch_shapes=[
            pltpu.SMEM(tile_row.shape, jnp.int32),
            pltpu.SMEM(tile_row.shape, jnp.int32),
            pltpu.SMEM(tile_col.shape, jnp.int32),
            pltpu.SMEM(tile_count.shape, jnp.int32),
            pltpu.VMEM(ratings.shape, ratings.dtype),
            pltpu.VMEM(row_mask.shape, jnp.int32),
            pltpu.VMEM((n_rep * rows, width), row_factors.dtype),
            pltpu.VMEM((cols, width), col_factors.dtype),
            pltpu.VMEM((n_strat - 1, phases, CAP, edge // phases, edge), ratings.dtype),
            pltpu.VMEM((n_strat - 1, meta_rows, edge), jnp.int32),
            pltpu.VMEM((n_strat, phases, CAP, edge // phases, edge), ratings.dtype),
            pltpu.VMEM((n_strat, meta_rows, edge), jnp.int32),
            pltpu.VMEM((phases, n_rep * rows // phases, width), jnp.float32),
            pltpu.VMEM((phases, n_rep * rows // phases, width), jnp.bfloat16),
            pltpu.VMEM((n_strat, CAP * edge, cols), jnp.bfloat16),
            pltpu.VMEM((n_strat, CAP * edge, width), jnp.bfloat16),
            pltpu.VMEM((rows, width), jnp.float32),
            pltpu.VMEM((n_rep - 2, rows, width), jnp.bfloat16),
            pltpu.VMEM((n_strat, CAP, edge, edge), jnp.float32),
            pltpu.VMEM((n_strat, CAP, edge, edge), jnp.float32),
            pltpu.VMEM((n_strat, CAP * edge, width), jnp.bfloat16),
            dma((4,)),
            dma((4,)),
            dma((n_rep - 1,)),
            dma((n_rep - 1,)),
            dma((n_strat - 1, phases)),
            dma((n_strat - 1, phases)),
            dma((n_strat - 1,)),
            dma((n_strat - 1,)),
            dma((turns,)),
            dma((turns,)),
            dma((turns * (n_rep - 2),)),
            dma((n_rep - 2, turns)),
            pltpu.SemaphoreType.REGULAR,
            pltpu.SemaphoreType.REGULAR((n_strat,)),
            pltpu.SemaphoreType.REGULAR((n_rep // 2,)),
        ],
        compiler_params=pltpu.CompilerParams(
            collective_id=0, has_side_effects=True
        ),
        name="gradient_pass",
    )(tile_owner.reshape(-1), tile_row, tile_col, tile_count, ratings, row_mask, row_factors, col_factors)
    row_grad, col_grad = (
        pltpu.with_memory_space_constraint(x, pltpu.VMEM) for x in (row_grad, col_grad)
    )
    anywhere = pl.BlockSpec(memory_space=pl.ANY)
    return pl.pallas_call(
        finish,
        out_shape=(
            jax.ShapeDtypeStruct((rows, width), jnp.float32),
            jax.ShapeDtypeStruct((cols, width), jnp.float32),
        ),
        in_specs=[anywhere] * 2,
        out_specs=(anywhere,) * 2,
        scratch_shapes=[dma((2,))],
        name="finish",
    )(row_grad, col_grad)


def solution(mesh):
    return jax.shard_map(
        on_device,
        mesh=mesh,
        in_specs=(
            P(("strat", "rep"), None, None),
            P(("strat", "rep"), None),
            P(("strat", "rep"), None),
            P(("strat", "rep")),
            P(("strat", "rep")),
            P(("strat", "rep")),
            P(("strat", "rep"), None),
            P(("strat", "rep"), None),
        ),
        out_specs=(P(("strat", "rep"), None), P(("strat", "rep"), None)),
        check_vma=False,
    )
```

```python
import functools

import jax
import jax.numpy as jnp
from jax import lax
from jax.experimental import pallas as pl
from jax.experimental.pallas import tpu as pltpu
from jax.sharding import PartitionSpec as P

CAP = 2
GROUP = 2
TURNS = 1


grad_scale = 0.0625
MESH = pl.DeviceIdType.MESH


def remote(src, dst, send_sem, recv_sem, **where):
    return pltpu.make_async_remote_copy(
        src_ref=src,
        dst_ref=dst,
        send_sem=send_sem,
        recv_sem=recv_sem,
        device_id=where,
        device_id_type=MESH,
    )


def kernel(
    n_strat, n_rep,
    owner_in, tile_row_in, tile_col_in, count_in, ratings, row_mask, row_factors, col_factors,
    row_out, col_out,
    owner, tile_row, tile_col, count,
    tiles, masks, row_all, col_all, send_vals, send_meta, recv_vals, recv_meta,
    row_acc, row_send, col_errors, row_picks, land_pair, land_far,
    predictions, keeps, col_picks,
    small_sem, local_sem, u_send, u_recv, v_send, v_recv, m_send, m_recv,
    p_send, p_recv, d_send, d_recv, ready, strat_in,
):
    held, edge = tiles.shape[0], tiles.shape[1]
    rows = row_factors.shape[0]
    n_row, n_col = row_all.shape[0] // edge, col_all.shape[0] // edge
    me_s, me_q = lax.axis_index("strat"), lax.axis_index("rep")
    pairs = n_rep // 2
    chip, side = me_q // 2, lax.rem(me_q, 2)
    partner = 2 * chip + 1 - side
    peers, own = n_strat - 1, n_strat - 1
    phases, part = send_vals.shape[1], send_vals.shape[3]
    turns = max(1, phases // 2)
    piece = rows // turns

    def rows_of(index):
        return pl.ds(pl.multiple_of(index * rows, rows), rows)

    def first_row(h):
        return h % 2 * rows + h // 2 * part if phases > 1 else 0

    def other(k, me):
        past = jnp.where(k >= me, 1, 0)
        return k + past, me - 1 + past

    def pick(blocks, same):
        wide = blocks.shape[1] // edge
        chosen = None
        for b, flag in enumerate(same):
            flag = jnp.concatenate([flag] * wide, axis=1)
            weight = jnp.broadcast_to(flag, (edge, wide * edge)).astype(blocks.dtype)
            part = blocks[b * edge : (b + 1) * edge, :] * weight
            chosen = part if chosen is None else chosen + part
        return chosen

    local = [
        pltpu.make_async_copy(row_mask, masks, local_sem.at[0]),
        pltpu.make_async_copy(ratings, tiles, local_sem.at[1]),
        pltpu.make_async_copy(row_factors, row_all.at[rows_of(me_q)], local_sem.at[2]),
        pltpu.make_async_copy(col_factors, col_all, local_sem.at[3]),
    ]
    small = [
        pltpu.make_async_copy(source, target, small_sem.at[i])
        for i, (source, target) in enumerate(
            [(owner_in, owner), (tile_row_in, tile_row), (tile_col_in, tile_col), (count_in, count)]
        )
    ]
    for copy in small + local[:2]:
        copy.start()

    barrier = pltpu.get_barrier_semaphore()

    def signal(semaphore, **where):
        pl.semaphore_signal(semaphore, inc=1, device_id=where, device_id_type=MESH)

    for k in range(pairs - 1):
        pair = other(k, chip)[0]
        signal(barrier, rep=2 * pair + 1)

        @pl.when(chip == 0)
        def _():
            signal(barrier, rep=2 * pair)

    signal(barrier, rep=partner)
    for k in range(peers):
        @pl.when(k >= me_s)
        def _():
            signal(barrier, strat=k + 1, rep=2 * chip)

    for copy in local[2:]:
        copy.start()

    @pl.when(side == 0)
    def _():
        pl.semaphore_wait(barrier, 2 * me_s + jnp.where(chip == 0, 1, 3))
        signal(ready, rep=partner)
        for k in range(peers):
            @pl.when(k < me_s)
            def _():
                for e in range(2):
                    signal(strat_in.at[me_s], strat=k, rep=2 * chip + e)

    far = [(k, e) for k in range(pairs - 1) for e in range(2)]

    def far_peer(k, e):
        target, slot = other(k, chip)
        return 2 * target + lax.rem(side + e, 2), 2 * slot + e

    u_copies = []
    for i, (k, e) in enumerate(far):
        peer, slot = far_peer(k, e)
        u_copies.append(
            remote(row_factors, row_all.at[rows_of(me_q)], u_send.at[i], u_recv.at[slot], rep=peer)
        )
    u_copies.append(
        remote(
            row_factors, row_all.at[rows_of(me_q)], u_send.at[len(far)], u_recv.at[len(far)],
            rep=partner,
        )
    )

    for copy in small:
        copy.wait()

    live = [p < count[0, 0] for p in range(held)]
    owners = [owner[p] for p in range(held)]
    plan = []
    for k in range(n_strat):
        dest = me_s if k == own else other(k, me_s)[0]
        seen = jnp.int32(0)
        flags = [[] for _ in range(CAP)]
        slot_ids = [[jnp.int32(0), jnp.int32(0)] for _ in range(CAP)]
        for p in range(held):
            here = jnp.where(jnp.logical_and(live[p], owners[p] == dest), 1, 0)
            for i in range(CAP):
                flag = jnp.where(seen == i, here, 0)
                flags[i].append(flag)
                slot_ids[i][0] += flag * tile_row[p]
                slot_ids[i][1] += flag * tile_col[p]
            seen = seen + here
        plan.append((flags, slot_ids))

    local[0].wait()
    for k in range(n_strat):
        flags, slot_ids = plan[k]
        meta = recv_meta.at[own] if k == own else send_meta.at[k]
        for i in range(CAP):
            row = masks[0:1, :] * flags[i][0]
            for p in range(1, held):
                row = row + masks[p : p + 1, :] * flags[i][p]
            meta[i : i + 1, :] = row
            for j in range(2):
                at = (1 + j) * CAP + i
                meta[at : at + 1, :] = jnp.full((1, edge), slot_ids[i][j], jnp.int32)
        meta[3 * CAP :, :] = jnp.zeros((meta.shape[0] - 3 * CAP, edge), jnp.int32)
    local[1].wait()
    for k in range(n_strat):
        flags, _ = plan[k]
        slots = recv_vals.at[own] if k == own else send_vals.at[k]
        for i in range(CAP):
            value = None
            for p in range(held):
                weight = jnp.full((edge, edge), flags[i][p].astype(jnp.float32)).astype(tiles.dtype)
                term = tiles[p] * weight
                value = term if value is None else value + term
            for h in range(phases):
                slots[h, i] = value[first_row(h) : first_row(h) + part]

    m_copies, v_copies = [], []
    for k in range(peers):
        dest, slot = other(k, me_s)
        m_copies.append(
            remote(send_meta.at[k], recv_meta.at[slot], m_send.at[k], m_recv.at[slot], strat=dest)
        )
        v_copies.append(
            [
                remote(
                    send_vals.at[k, h], recv_vals.at[slot, h], v_send.at[k, h], v_recv.at[slot, h],
                    strat=dest,
                )
                for h in range(phases)
            ]
        )
    @pl.when(side == 1)
    def _():
        pl.semaphore_wait(ready, 1)

    @pl.when(chip > 0)
    def _():
        for e in range(2):
            u_copies[e].start()

    for k in range(peers):
        pl.when(k < me_s)(m_copies[k].start)

    @pl.when(me_s > 0)
    def _():
        for copy in v_copies[0]:
            copy.start()

    @pl.when(side == 1)
    def _():
        pl.semaphore_wait(barrier, n_rep - 1)
        signal(ready, rep=partner)

    @pl.when(side == 0)
    def _():
        pl.semaphore_wait(ready, 1)

    @pl.when(chip == 0)
    def _():
        for e in range(2):
            u_copies[e].start()

    for copy in u_copies[2:]:
        copy.start()

    for k in list(range(1, peers))[::-1]:
        @pl.when(k < me_s)
        def _():
            for copy in v_copies[k]:
                copy.start()

    for k in range(peers):
        @pl.when(k >= me_s)
        def _():
            pl.semaphore_wait(strat_in.at[k + 1], 1)
            m_copies[k].start()
            for copy in v_copies[k]:
                copy.start()

    order = [own] + list(range(peers))

    def m_at(slot):
        return remote(
            send_meta.at[slot], recv_meta.at[slot], m_send.at[slot], m_recv.at[slot],
            strat=other(slot, me_s)[0],
        )

    def v_at(slot, h):
        return remote(
            send_vals.at[slot, h], recv_vals.at[slot, h], v_send.at[slot, h], v_recv.at[slot, h],
            strat=other(slot, me_s)[0],
        )

    def u_at(slot):
        return remote(
            row_factors, row_all.at[rows_of(me_q)], u_send.at[slot], u_recv.at[slot], rep=partner
        )

    for k in range(peers):
        m_at(k).wait_recv()
    local[2].wait()
    local[3].wait()
    for i in range(n_rep - 1):
        u_at(i).wait_recv()

    def flags_of(r):
        meta = recv_meta[r].astype(jnp.float32)
        in_row, in_col = [], []
        for k in range(CAP):
            row_id, col_id = (meta[(1 + i) * CAP + k : (1 + i) * CAP + k + 1, :] for i in range(2))
            in_row.append([jnp.where(row_id == b, 1.0, 0.0) for b in range(n_row)])
            in_col.append([jnp.where(col_id == c, 1.0, 0.0) for c in range(n_col)])
        return meta, in_row, in_col

    for r in order:
        meta, in_row, in_col = flags_of(r)
        keep = meta.T
        for k in range(CAP):
            row_pick, col_pick = pick(row_all, in_row[k]), pick(col_all, in_col[k])
            row_picks[r, k * edge : (k + 1) * edge, :] = row_pick
            col_picks[r, k * edge : (k + 1) * edge, :] = col_pick
            predictions[r, k] = lax.dot_general(
                row_pick, col_pick, (((1,), (1,)), ((), ())), preferred_element_type=jnp.float32
            )
            keeps[r, k] = jnp.broadcast_to(keep[:, k : k + 1], (edge, edge))

    def add_columns():
        total = None
        for r in order:
            term = lax.dot_general(
                col_errors[r], row_picks[r], (((0,), (0,)), ((), ())),
                preferred_element_type=jnp.float32,
            )
            total = term if total is None else total + term
        col_out[...] = total * grad_scale

    d_copies, p_copies = [], []
    for h in range(phases):
        for at in range(0, n_strat, GROUP):
            group = order[at : at + GROUP]
            for r in group:
                if r != own:
                    v_at(r, h).wait_recv()
            lefts = []
            for r in group:
                _, row_same, in_col = flags_of(r)
                errors = []
                for k in range(CAP):
                    here = slice(first_row(h), first_row(h) + part)
                    error = keeps[r, k, here, :] * (
                        predictions[r, k, here, :] - recv_vals[r, h, k].astype(jnp.float32)
                    )
                    errors.append(error)
                    first = k * edge + first_row(h)
                    for c in range(n_col):
                        col_errors[r, first : first + part, c * edge : (c + 1) * edge] = (
                            error * in_col[k][c]
                        ).astype(jnp.bfloat16)
                lefts.append(
                    jnp.concatenate(
                        [
                            jnp.concatenate(
                                [(errors[k] * row_same[k][b]).astype(jnp.bfloat16) for k in range(CAP)],
                                axis=1,
                            )
                            for b in range(n_row)
                        ],
                        axis=0,
                    )
                )
            term = jnp.dot(
                jnp.concatenate(lefts, axis=1),
                jnp.concatenate([col_picks[r] for r in group], axis=0),
                preferred_element_type=jnp.float32,
            )
            if at:
                term = row_acc[h] + term
            row_acc[h] = term
            if group[-1] == order[-1]:
                row_send[h] = term.astype(row_send.dtype)

        turn = h // 2
        within = pl.ds(turn * piece, piece)
        for k in range(pairs - 1):
            for e in [lax.rem(side + h, 2)] if phases > 1 else range(2):
                peer, slot = far_peer(k, e)
                start = peer // 2 * piece if phases > 1 else peer * piece
                i = len(d_copies)
                copy = remote(
                    row_send.at[h, pl.ds(pl.multiple_of(start, piece), piece)],
                    land_far.at[slot, within], d_send.at[i], d_recv.at[slot, turn], rep=peer,
                )
                copy.start()
                d_copies.append(copy)
        if phases == 1 or h % 2:
            start = chip * piece if phases > 1 else partner * piece
            which = 2 * turn + 1 - side if phases > 1 else 0
            p_copies.append(
                remote(
                    row_acc.at[which, pl.ds(pl.multiple_of(start, piece), piece)],
                    land_pair.at[within], p_send.at[turn], p_recv.at[turn], rep=partner,
                )
            )
        if phases == 1:
            p_copies[turn].start()
        elif h % 2:
            pl.when(side == 0)(p_copies[turn].start)
        else:
            pl.when(side == 1)(
                remote(
                    row_acc.at[h, pl.ds(pl.multiple_of(chip * piece, piece), piece)],
                    land_pair.at[within], p_send.at[turn], p_recv.at[turn], rep=partner,
                ).start
            )
    add_columns()
    for turn in range(turns):
        within = pl.ds(turn * piece, piece)
        p_copies[turn].wait_recv()
        which, start = (2 * turn + side, chip * piece) if phases > 1 else (0, me_q * piece)
        mine = row_acc[which, pl.ds(pl.multiple_of(start, piece), piece), :] + land_pair[within, :]
        for i in range(len(far)):
            remote(
                row_send.at[0, pl.ds(0, piece)], land_far.at[i, within], d_send.at[i],
                d_recv.at[i, turn], rep=partner,
            ).wait_recv()
            mine = mine + land_far[i, within, :].astype(jnp.float32)
        row_out[within, :] = mine * grad_scale

    for copy in u_copies + m_copies + sum(v_copies, []) + d_copies + p_copies:
        copy.wait_send()


def finish(row_in, col_in, row_out, col_out, sems):
    copies = [
        pltpu.make_async_copy(col_in, col_out, sems.at[0]),
        pltpu.make_async_copy(row_in, row_out, sems.at[1]),
    ]
    for copy in copies:
        copy.start()
    for copy in copies:
        copy.wait()


def on_device(
    ratings, row_mask, tile_owner, tile_row, tile_col, tile_count, row_factors, col_factors
):
    n_strat, n_rep = lax.axis_size("strat"), lax.axis_size("rep")
    edge = ratings.shape[1]
    rows, width = row_factors.shape
    cols = col_factors.shape[0]
    meta_rows = 8
    phases = 1
    if edge == 2 * rows and rows % (16 * TURNS) == 0:
        phases = 2 * TURNS
    turns = max(1, phases // 2)
    tile_count = tile_count.reshape(1, 1)
    hbm = pl.BlockSpec(memory_space=pltpu.HBM)
    vmem = pl.BlockSpec(memory_space=pltpu.VMEM)
    dma = pltpu.SemaphoreType.DMA
    row_grad, col_grad = pl.pallas_call(
        functools.partial(kernel, n_strat, n_rep),
        out_shape=(
            pltpu.VMEM((rows, width), jnp.float32),
            pltpu.VMEM((cols, width), jnp.float32),
        ),
        in_specs=[hbm] * 8,
        out_specs=(vmem, vmem),
        scratch_shapes=[
            pltpu.SMEM(tile_row.shape, jnp.int32),
            pltpu.SMEM(tile_row.shape, jnp.int32),
            pltpu.SMEM(tile_col.shape, jnp.int32),
            pltpu.SMEM(tile_count.shape, jnp.int32),
            pltpu.VMEM(ratings.shape, ratings.dtype),
            pltpu.VMEM(row_mask.shape, jnp.int32),
            pltpu.VMEM((n_rep * rows, width), row_factors.dtype),
            pltpu.VMEM((cols, width), col_factors.dtype),
            pltpu.VMEM((n_strat - 1, phases, CAP, edge // phases, edge), ratings.dtype),
            pltpu.VMEM((n_strat - 1, meta_rows, edge), jnp.int32),
            pltpu.VMEM((n_strat, phases, CAP, edge // phases, edge), ratings.dtype),
            pltpu.VMEM((n_strat, meta_rows, edge), jnp.int32),
            pltpu.VMEM((phases, n_rep * rows // phases, width), jnp.float32),
            pltpu.VMEM((phases, n_rep * rows // phases, width), jnp.bfloat16),
            pltpu.VMEM((n_strat, CAP * edge, cols), jnp.bfloat16),
            pltpu.VMEM((n_strat, CAP * edge, width), jnp.bfloat16),
            pltpu.VMEM((rows, width), jnp.float32),
            pltpu.VMEM((n_rep - 2, rows, width), jnp.bfloat16),
            pltpu.VMEM((n_strat, CAP, edge, edge), jnp.float32),
            pltpu.VMEM((n_strat, CAP, edge, edge), jnp.float32),
            pltpu.VMEM((n_strat, CAP * edge, width), jnp.bfloat16),
            dma((4,)),
            dma((4,)),
            dma((n_rep - 1,)),
            dma((n_rep - 1,)),
            dma((n_strat - 1, phases)),
            dma((n_strat - 1, phases)),
            dma((n_strat - 1,)),
            dma((n_strat - 1,)),
            dma((turns,)),
            dma((turns,)),
            dma((turns * (n_rep - 2),)),
            dma((n_rep - 2, turns)),
            pltpu.SemaphoreType.REGULAR,
            pltpu.SemaphoreType.REGULAR((n_strat,)),
        ],
        compiler_params=pltpu.CompilerParams(
            collective_id=0, has_side_effects=True
        ),
        name="gradient_pass",
    )(tile_owner.reshape(-1), tile_row, tile_col, tile_count, ratings, row_mask, row_factors, col_factors)
    row_grad, col_grad = (
        pltpu.with_memory_space_constraint(x, pltpu.VMEM) for x in (row_grad, col_grad)
    )
    anywhere = pl.BlockSpec(memory_space=pl.ANY)
    return pl.pallas_call(
        finish,
        out_shape=(
            jax.ShapeDtypeStruct((rows, width), jnp.float32),
            jax.ShapeDtypeStruct((cols, width), jnp.float32),
        ),
        in_specs=[anywhere] * 2,
        out_specs=(anywhere,) * 2,
        scratch_shapes=[dma((2,))],
        name="finish",
    )(row_grad, col_grad)


def solution(mesh):
    return jax.shard_map(
        on_device,
        mesh=mesh,
        in_specs=(
            P(("strat", "rep"), None, None),
            P(("strat", "rep"), None),
            P(("strat", "rep"), None),
            P(("strat", "rep")),
            P(("strat", "rep")),
            P(("strat", "rep")),
            P(("strat", "rep"), None),
            P(("strat", "rep"), None),
        ),
        out_specs=(P(("strat", "rep"), None), P(("strat", "rep"), None)),
        check_vma=False,
    )
```

```python
import functools

import jax
import jax.numpy as jnp
from jax import lax
from jax.experimental import pallas as pl
from jax.experimental.pallas import tpu as pltpu
from jax.sharding import PartitionSpec as P

CAP = 2
GROUP = 2
TURNS = 1


grad_scale = 0.0625
MESH = pl.DeviceIdType.MESH


def remote(src, dst, send_sem, recv_sem, **where):
    return pltpu.make_async_remote_copy(
        src_ref=src,
        dst_ref=dst,
        send_sem=send_sem,
        recv_sem=recv_sem,
        device_id=where,
        device_id_type=MESH,
    )


def kernel(
    n_strat, n_rep,
    owner_in, tile_row_in, tile_col_in, count_in, ratings, row_mask, row_factors, col_factors,
    row_out, col_out,
    owner, tile_row, tile_col, count,
    tiles, masks, row_all, col_all, send_vals, send_meta, recv_vals, recv_meta,
    row_acc, row_send, col_errors, row_picks, land_pair, land_far,
    predictions, keeps, col_picks,
    small_sem, local_sem, u_send, u_recv, v_send, v_recv, m_send, m_recv,
    p_send, p_recv, d_send, d_recv, ready, strat_in,
):
    held, edge = tiles.shape[0], tiles.shape[1]
    rows = row_factors.shape[0]
    n_row, n_col = row_all.shape[0] // edge, col_all.shape[0] // edge
    me_s, me_q = lax.axis_index("strat"), lax.axis_index("rep")
    pairs = n_rep // 2
    chip, side = me_q // 2, lax.rem(me_q, 2)
    partner = 2 * chip + 1 - side
    peers, own = n_strat - 1, n_strat - 1
    phases, part = send_vals.shape[1], send_vals.shape[3]
    turns = max(1, phases // 2)
    piece = rows // turns

    def rows_of(index):
        return pl.ds(pl.multiple_of(index * rows, rows), rows)

    def first_row(h):
        return h % 2 * rows + h // 2 * part if phases > 1 else 0

    def other(k, me):
        past = jnp.where(k >= me, 1, 0)
        return k + past, me - 1 + past

    def pick(blocks, same):
        wide = blocks.shape[1] // edge
        chosen = None
        for b, flag in enumerate(same):
            flag = jnp.concatenate([flag] * wide, axis=1)
            weight = jnp.broadcast_to(flag, (edge, wide * edge)).astype(blocks.dtype)
            part = blocks[b * edge : (b + 1) * edge, :]
            chosen = part if chosen is None else jnp.where(weight > 0, part, chosen)
        return chosen

    local = [
        pltpu.make_async_copy(row_mask, masks, local_sem.at[0]),
        pltpu.make_async_copy(ratings, tiles, local_sem.at[1]),
        pltpu.make_async_copy(row_factors, row_all.at[rows_of(me_q)], local_sem.at[2]),
        pltpu.make_async_copy(col_factors, col_all, local_sem.at[3]),
    ]
    small = [
        pltpu.make_async_copy(source, target, small_sem.at[i])
        for i, (source, target) in enumerate(
            [(owner_in, owner), (tile_row_in, tile_row), (tile_col_in, tile_col), (count_in, count)]
        )
    ]
    barrier = pltpu.get_barrier_semaphore()

    def signal(semaphore, **where):
        pl.semaphore_signal(semaphore, inc=1, device_id=where, device_id_type=MESH)

    for k in range(pairs - 1):
        pair = other(k, chip)[0]
        signal(barrier, rep=2 * pair + 1)

        @pl.when(chip == 0)
        def _():
            signal(barrier, rep=2 * pair)

    signal(barrier, rep=partner)
    for k in range(peers):
        @pl.when(k >= me_s)
        def _():
            signal(barrier, strat=k + 1, rep=2 * chip)

    for copy in small + local[:2]:
        copy.start()

    for copy in local[2:]:
        copy.start()

    @pl.when(side == 0)
    def _():
        pl.semaphore_wait(barrier, 2 * me_s + jnp.where(chip == 0, 1, 3))
        signal(ready, rep=partner)
        for k in range(peers):
            @pl.when(k < me_s)
            def _():
                for e in range(2):
                    signal(strat_in.at[me_s], strat=k, rep=2 * chip + e)

    far = [(k, e) for k in range(pairs - 1) for e in range(2)]

    def far_peer(k, e):
        target, slot = other(k, chip)
        return 2 * target + lax.rem(side + e, 2), 2 * slot + e

    u_copies = []
    for i, (k, e) in enumerate(far):
        peer, slot = far_peer(k, e)
        u_copies.append(
            remote(row_factors, row_all.at[rows_of(me_q)], u_send.at[i], u_recv.at[slot], rep=peer)
        )
    u_copies.append(
        remote(
            row_factors, row_all.at[rows_of(me_q)], u_send.at[len(far)], u_recv.at[len(far)],
            rep=partner,
        )
    )

    for copy in small:
        copy.wait()

    live = [p < count[0, 0] for p in range(held)]
    owners = [owner[p] for p in range(held)]
    plan = []
    for k in range(n_strat):
        dest = me_s if k == own else other(k, me_s)[0]
        seen = jnp.int32(0)
        flags = [[] for _ in range(CAP)]
        slot_ids = [[jnp.int32(0), jnp.int32(0)] for _ in range(CAP)]
        for p in range(held):
            here = jnp.where(jnp.logical_and(live[p], owners[p] == dest), 1, 0)
            for i in range(CAP):
                flag = jnp.where(seen == i, here, 0)
                flags[i].append(flag)
                slot_ids[i][0] += flag * tile_row[p]
                slot_ids[i][1] += flag * tile_col[p]
            seen = seen + here
        plan.append((flags, slot_ids))

    local[0].wait()
    for k in range(n_strat):
        flags, slot_ids = plan[k]
        meta = recv_meta.at[own] if k == own else send_meta.at[k]
        for i in range(CAP):
            row = masks[0:1, :] * flags[i][0]
            for p in range(1, held):
                row = row + masks[p : p + 1, :] * flags[i][p]
            meta[i : i + 1, :] = row
            for j in range(2):
                at = (1 + j) * CAP + i
                meta[at : at + 1, :] = jnp.full((1, edge), slot_ids[i][j], jnp.int32)
        meta[3 * CAP :, :] = jnp.zeros((meta.shape[0] - 3 * CAP, edge), jnp.int32)
    local[1].wait()
    for k in range(n_strat):
        flags, _ = plan[k]
        slots = recv_vals.at[own] if k == own else send_vals.at[k]
        for i in range(CAP):
            value = None
            for p in range(held):
                weight = jnp.full((edge, edge), flags[i][p].astype(jnp.float32)).astype(tiles.dtype)
                term = tiles[p] * weight
                value = term if value is None else value + term
            for h in range(phases):
                slots[h, i] = value[first_row(h) : first_row(h) + part]

    m_copies, v_copies = [], []
    for k in range(peers):
        dest, slot = other(k, me_s)
        m_copies.append(
            remote(send_meta.at[k], recv_meta.at[slot], m_send.at[k], m_recv.at[slot], strat=dest)
        )
        v_copies.append(
            [
                remote(
                    send_vals.at[k, h], recv_vals.at[slot, h], v_send.at[k, h], v_recv.at[slot, h],
                    strat=dest,
                )
                for h in range(phases)
            ]
        )
    @pl.when(side == 1)
    def _():
        pl.semaphore_wait(ready, 1)

    @pl.when(chip > 0)
    def _():
        for e in range(2):
            u_copies[e].start()

    for k in range(peers):
        pl.when(k < me_s)(m_copies[k].start)

    @pl.when(me_s > 0)
    def _():
        for copy in v_copies[0]:
            copy.start()

    @pl.when(side == 1)
    def _():
        pl.semaphore_wait(barrier, n_rep - 1)
        signal(ready, rep=partner)

    @pl.when(side == 0)
    def _():
        pl.semaphore_wait(ready, 1)

    @pl.when(chip == 0)
    def _():
        for e in range(2):
            u_copies[e].start()

    for copy in u_copies[2:]:
        copy.start()

    for k in list(range(1, peers))[::-1]:
        @pl.when(k < me_s)
        def _():
            for copy in v_copies[k]:
                copy.start()

    for k in range(peers):
        @pl.when(k == me_s)
        def _():
            pl.semaphore_wait(strat_in.at[k + 1], 1)
            m_copies[k].start()
            v_copies[k][0].start()

    for k in range(peers):
        @pl.when(k > me_s)
        def _():
            pl.semaphore_wait(strat_in.at[k + 1], 1)
            m_copies[k].start()
            v_copies[k][0].start()

    for h in range(1, phases):
        for k in range(peers)[::-1]:
            @pl.when(k >= me_s)
            def _():
                v_copies[k][h].start()

    order = [own] + list(range(peers))

    def m_at(slot):
        return remote(
            send_meta.at[slot], recv_meta.at[slot], m_send.at[slot], m_recv.at[slot],
            strat=other(slot, me_s)[0],
        )

    def v_at(slot, h):
        return remote(
            send_vals.at[slot, h], recv_vals.at[slot, h], v_send.at[slot, h], v_recv.at[slot, h],
            strat=other(slot, me_s)[0],
        )

    def u_at(slot):
        return remote(
            row_factors, row_all.at[rows_of(me_q)], u_send.at[slot], u_recv.at[slot], rep=partner
        )

    for k in range(peers):
        m_at(k).wait_recv()
    local[2].wait()
    local[3].wait()
    def flags_of(r):
        meta = recv_meta[r].astype(jnp.float32)
        in_row, in_col = [], []
        for k in range(CAP):
            row_id, col_id = (meta[(1 + i) * CAP + k : (1 + i) * CAP + k + 1, :] for i in range(2))
            in_row.append([jnp.where(row_id == b, 1.0, 0.0) for b in range(n_row)])
            in_col.append([jnp.where(col_id == c, 1.0, 0.0) for c in range(n_col)])
        return meta, in_row, in_col

    for r in order:
        meta, _, in_col = flags_of(r)
        keep = meta.T
        for k in range(CAP):
            col_picks[r, k * edge : (k + 1) * edge, :] = pick(col_all, in_col[k])
            keeps[r, k] = jnp.broadcast_to(keep[:, k : k + 1], (edge, edge))

    for i in range(n_rep - 1):
        u_at(i).wait_recv()

    for r in order:
        _, in_row, _ = flags_of(r)
        for k in range(CAP):
            row_pick = pick(row_all, in_row[k])
            row_picks[r, k * edge : (k + 1) * edge, :] = row_pick
            predictions[r, k] = lax.dot_general(
                row_pick, col_picks[r, k * edge : (k + 1) * edge, :], (((1,), (1,)), ((), ())),
                preferred_element_type=jnp.float32,
            )

    def add_columns():
        total = None
        for r in order:
            term = lax.dot_general(
                col_errors[r], row_picks[r], (((0,), (0,)), ((), ())),
                preferred_element_type=jnp.float32,
            )
            total = term if total is None else total + term
        col_out[...] = total * grad_scale

    d_copies, p_copies = [], []
    for h in range(phases):
        for at in range(0, n_strat, GROUP):
            group = order[at : at + GROUP]
            for r in group:
                if r != own:
                    v_at(r, h).wait_recv()
            lefts = []
            for r in group:
                _, row_same, in_col = flags_of(r)
                errors = []
                for k in range(CAP):
                    here = slice(first_row(h), first_row(h) + part)
                    error = keeps[r, k, here, :] * (
                        predictions[r, k, here, :] - recv_vals[r, h, k].astype(jnp.float32)
                    )
                    errors.append(error)
                    first = k * edge + first_row(h)
                    for c in range(n_col):
                        col_errors[r, first : first + part, c * edge : (c + 1) * edge] = (
                            error * in_col[k][c]
                        ).astype(jnp.bfloat16)
                lefts.append(
                    jnp.concatenate(
                        [
                            jnp.concatenate(
                                [(errors[k] * row_same[k][b]).astype(jnp.bfloat16) for k in range(CAP)],
                                axis=1,
                            )
                            for b in range(n_row)
                        ],
                        axis=0,
                    )
                )
            term = jnp.dot(
                jnp.concatenate(lefts, axis=1),
                jnp.concatenate([col_picks[r] for r in group], axis=0),
                preferred_element_type=jnp.float32,
            )
            if at:
                term = row_acc[h] + term
            row_acc[h] = term
            if group[-1] == order[-1]:
                row_send[h] = term.astype(row_send.dtype)

        turn = h // 2
        within = pl.ds(turn * piece, piece)
        for k in range(pairs - 1):
            for e in [lax.rem(side + h, 2)] if phases > 1 else range(2):
                peer, slot = far_peer(k, e)
                start = peer // 2 * piece if phases > 1 else peer * piece
                i = len(d_copies)
                copy = remote(
                    row_send.at[h, pl.ds(pl.multiple_of(start, piece), piece)],
                    land_far.at[slot, within], d_send.at[i], d_recv.at[slot, turn], rep=peer,
                )
                copy.start()
                d_copies.append(copy)
        if phases == 1 or h % 2:
            start = chip * piece if phases > 1 else partner * piece
            which = 2 * turn + 1 - side if phases > 1 else 0
            p_copies.append(
                remote(
                    row_acc.at[which, pl.ds(pl.multiple_of(start, piece), piece)],
                    land_pair.at[within], p_send.at[turn], p_recv.at[turn], rep=partner,
                )
            )
        if phases == 1:
            p_copies[turn].start()
        elif h % 2:
            pl.when(side == 0)(p_copies[turn].start)
        else:
            pl.when(side == 1)(
                remote(
                    row_acc.at[h, pl.ds(pl.multiple_of(chip * piece, piece), piece)],
                    land_pair.at[within], p_send.at[turn], p_recv.at[turn], rep=partner,
                ).start
            )
    add_columns()
    for turn in range(turns):
        within = pl.ds(turn * piece, piece)
        p_copies[turn].wait_recv()
        which, start = (2 * turn + side, chip * piece) if phases > 1 else (0, me_q * piece)
        mine = row_acc[which, pl.ds(pl.multiple_of(start, piece), piece), :] + land_pair[within, :]
        for i in range(len(far)):
            remote(
                row_send.at[0, pl.ds(0, piece)], land_far.at[i, within], d_send.at[i],
                d_recv.at[i, turn], rep=partner,
            ).wait_recv()
            mine = mine + land_far[i, within, :].astype(jnp.float32)
        row_out[within, :] = mine * grad_scale

    for copy in u_copies + m_copies + sum(v_copies, []) + d_copies + p_copies:
        copy.wait_send()


def finish(row_in, col_in, row_out, col_out, sems):
    copies = [
        pltpu.make_async_copy(col_in, col_out, sems.at[0]),
        pltpu.make_async_copy(row_in, row_out, sems.at[1]),
    ]
    for copy in copies:
        copy.start()
    for copy in copies:
        copy.wait()


def on_device(
    ratings, row_mask, tile_owner, tile_row, tile_col, tile_count, row_factors, col_factors
):
    n_strat, n_rep = lax.axis_size("strat"), lax.axis_size("rep")
    edge = ratings.shape[1]
    rows, width = row_factors.shape
    cols = col_factors.shape[0]
    meta_rows = 8
    phases = 1
    if edge == 2 * rows and rows % (16 * TURNS) == 0:
        phases = 2 * TURNS
    turns = max(1, phases // 2)
    tile_count = tile_count.reshape(1, 1)
    hbm = pl.BlockSpec(memory_space=pltpu.HBM)
    vmem = pl.BlockSpec(memory_space=pltpu.VMEM)
    dma = pltpu.SemaphoreType.DMA
    row_grad, col_grad = pl.pallas_call(
        functools.partial(kernel, n_strat, n_rep),
        out_shape=(
            pltpu.VMEM((rows, width), jnp.float32),
            pltpu.VMEM((cols, width), jnp.float32),
        ),
        in_specs=[hbm] * 8,
        out_specs=(vmem, vmem),
        scratch_shapes=[
            pltpu.SMEM(tile_row.shape, jnp.int32),
            pltpu.SMEM(tile_row.shape, jnp.int32),
            pltpu.SMEM(tile_col.shape, jnp.int32),
            pltpu.SMEM(tile_count.shape, jnp.int32),
            pltpu.VMEM(ratings.shape, ratings.dtype),
            pltpu.VMEM(row_mask.shape, jnp.int32),
            pltpu.VMEM((n_rep * rows, width), row_factors.dtype),
            pltpu.VMEM((cols, width), col_factors.dtype),
            pltpu.VMEM((n_strat - 1, phases, CAP, edge // phases, edge), ratings.dtype),
            pltpu.VMEM((n_strat - 1, meta_rows, edge), jnp.int32),
            pltpu.VMEM((n_strat, phases, CAP, edge // phases, edge), ratings.dtype),
            pltpu.VMEM((n_strat, meta_rows, edge), jnp.int32),
            pltpu.VMEM((phases, n_rep * rows // phases, width), jnp.float32),
            pltpu.VMEM((phases, n_rep * rows // phases, width), jnp.bfloat16),
            pltpu.VMEM((n_strat, CAP * edge, cols), jnp.bfloat16),
            pltpu.VMEM((n_strat, CAP * edge, width), jnp.bfloat16),
            pltpu.VMEM((rows, width), jnp.float32),
            pltpu.VMEM((n_rep - 2, rows, width), jnp.bfloat16),
            pltpu.VMEM((n_strat, CAP, edge, edge), jnp.float32),
            pltpu.VMEM((n_strat, CAP, edge, edge), jnp.float32),
            pltpu.VMEM((n_strat, CAP * edge, width), jnp.bfloat16),
            dma((4,)),
            dma((4,)),
            dma((n_rep - 1,)),
            dma((n_rep - 1,)),
            dma((n_strat - 1, phases)),
            dma((n_strat - 1, phases)),
            dma((n_strat - 1,)),
            dma((n_strat - 1,)),
            dma((turns,)),
            dma((turns,)),
            dma((turns * (n_rep - 2),)),
            dma((n_rep - 2, turns)),
            pltpu.SemaphoreType.REGULAR,
            pltpu.SemaphoreType.REGULAR((n_strat,)),
        ],
        compiler_params=pltpu.CompilerParams(
            collective_id=0, has_side_effects=True
        ),
        name="gradient_pass",
    )(tile_owner.reshape(-1), tile_row, tile_col, tile_count, ratings, row_mask, row_factors, col_factors)
    row_grad, col_grad = (
        pltpu.with_memory_space_constraint(x, pltpu.VMEM) for x in (row_grad, col_grad)
    )
    anywhere = pl.BlockSpec(memory_space=pl.ANY)
    return pl.pallas_call(
        finish,
        out_shape=(
            jax.ShapeDtypeStruct((rows, width), jnp.float32),
            jax.ShapeDtypeStruct((cols, width), jnp.float32),
        ),
        in_specs=[anywhere] * 2,
        out_specs=(anywhere,) * 2,
        scratch_shapes=[dma((2,))],
        name="finish",
    )(row_grad, col_grad)


def solution(mesh):
    return jax.shard_map(
        on_device,
        mesh=mesh,
        in_specs=(
            P(("strat", "rep"), None, None),
            P(("strat", "rep"), None),
            P(("strat", "rep"), None),
            P(("strat", "rep")),
            P(("strat", "rep")),
            P(("strat", "rep")),
            P(("strat", "rep"), None),
            P(("strat", "rep"), None),
        ),
        out_specs=(P(("strat", "rep"), None), P(("strat", "rep"), None)),
        check_vma=False,
    )
```

```python
import functools

import jax
import jax.numpy as jnp
from jax import lax
from jax.experimental import pallas as pl
from jax.experimental.pallas import tpu as pltpu
from jax.sharding import PartitionSpec as P

CAP = 2
GROUP = 4
GROUP = 4
TURNS = 1


grad_scale = 0.0625
MESH = pl.DeviceIdType.MESH


def remote(src, dst, send_sem, recv_sem, **where):
    return pltpu.make_async_remote_copy(
        src_ref=src,
        dst_ref=dst,
        send_sem=send_sem,
        recv_sem=recv_sem,
        device_id=where,
        device_id_type=MESH,
    )


def kernel(
    n_strat, n_rep,
    owner_in, tile_row_in, tile_col_in, count_in, ratings, row_mask, row_factors, col_factors,
    row_out, col_out,
    owner, tile_row, tile_col, count,
    tiles, masks, row_all, col_all, send_vals, send_meta, recv_vals, recv_meta,
    row_acc, row_send, all_errors, row_picks, land_pair, land_far,
    predictions, keeps, col_picks,
    small_sem, local_sem, u_send, u_recv, v_send, v_recv, m_send, m_recv,
    p_send, p_recv, d_send, d_recv, ready, strat_in,
):
    held, edge = tiles.shape[0], tiles.shape[1]
    rows = row_factors.shape[0]
    n_row, n_col = row_all.shape[0] // edge, col_all.shape[0] // edge
    me_s, me_q = lax.axis_index("strat"), lax.axis_index("rep")
    pairs = n_rep // 2
    chip, side = me_q // 2, lax.rem(me_q, 2)
    partner = 2 * chip + 1 - side
    peers, own = n_strat - 1, n_strat - 1
    phases, part = send_vals.shape[1], send_vals.shape[3]
    turns = max(1, phases // 2)
    piece = rows // turns

    def rows_of(index):
        return pl.ds(pl.multiple_of(index * rows, rows), rows)

    def first_row(h):
        return h % 2 * rows + h // 2 * part if phases > 1 else 0

    def other(k, me):
        past = jnp.where(k >= me, 1, 0)
        return k + past, me - 1 + past

    def pick(blocks, same):
        wide = blocks.shape[1] // edge
        chosen = None
        for b, flag in enumerate(same):
            flag = jnp.concatenate([flag] * wide, axis=1)
            weight = jnp.broadcast_to(flag, (edge, wide * edge)).astype(blocks.dtype)
            part = blocks[b * edge : (b + 1) * edge, :]
            chosen = part if chosen is None else jnp.where(weight > 0, part, chosen)
        return chosen

    local = [
        pltpu.make_async_copy(row_mask, masks, local_sem.at[0]),
        pltpu.make_async_copy(ratings, tiles, local_sem.at[1]),
        pltpu.make_async_copy(row_factors, row_all.at[rows_of(me_q)], local_sem.at[2]),
        pltpu.make_async_copy(col_factors, col_all, local_sem.at[3]),
    ]
    small = [
        pltpu.make_async_copy(source, target, small_sem.at[i])
        for i, (source, target) in enumerate(
            [(owner_in, owner), (tile_row_in, tile_row), (tile_col_in, tile_col), (count_in, count)]
        )
    ]
    barrier = pltpu.get_barrier_semaphore()

    def signal(semaphore, **where):
        pl.semaphore_signal(semaphore, inc=1, device_id=where, device_id_type=MESH)

    for k in range(pairs - 1):
        pair = other(k, chip)[0]
        signal(barrier, rep=2 * pair + 1)

        @pl.when(chip == 0)
        def _():
            signal(barrier, rep=2 * pair)

    signal(barrier, rep=partner)
    for k in range(peers):
        @pl.when(k >= me_s)
        def _():
            signal(barrier, strat=k + 1, rep=2 * chip)

    for copy in small + local[:2]:
        copy.start()

    for copy in local[2:]:
        copy.start()

    @pl.when(side == 0)
    def _():
        pl.semaphore_wait(barrier, 2 * me_s + jnp.where(chip == 0, 1, 3))
        signal(ready, rep=partner)
        for k in range(peers):
            @pl.when(k < me_s)
            def _():
                for e in range(2):
                    signal(strat_in.at[me_s], strat=k, rep=2 * chip + e)

    far = [(k, e) for k in range(pairs - 1) for e in range(2)]

    def far_peer(k, e):
        target, slot = other(k, chip)
        return 2 * target + lax.rem(side + e, 2), 2 * slot + e

    own_rows = row_all.at[rows_of(me_q)]
    u_copies = []
    for i, (k, e) in enumerate(far):
        peer, slot = far_peer(k, e)
        u_copies.append(
            remote(own_rows, own_rows, u_send.at[i], u_recv.at[slot], rep=peer)
        )
    u_copies.append(
        remote(
            own_rows, own_rows, u_send.at[len(far)], u_recv.at[len(far)], rep=partner,
        )
    )

    for copy in small:
        copy.wait()

    live = [p < count[0, 0] for p in range(held)]
    owners = [owner[p] for p in range(held)]
    plan = []
    for k in range(n_strat):
        dest = me_s if k == own else other(k, me_s)[0]
        seen = jnp.int32(0)
        flags = [[] for _ in range(CAP)]
        slot_ids = [[jnp.int32(0), jnp.int32(0)] for _ in range(CAP)]
        for p in range(held):
            here = jnp.where(jnp.logical_and(live[p], owners[p] == dest), 1, 0)
            for i in range(CAP):
                flag = jnp.where(seen == i, here, 0)
                flags[i].append(flag)
                slot_ids[i][0] += flag * tile_row[p]
                slot_ids[i][1] += flag * tile_col[p]
            seen = seen + here
        plan.append((flags, slot_ids))

    local[0].wait()
    for k in range(n_strat):
        flags, slot_ids = plan[k]
        meta = recv_meta.at[own] if k == own else send_meta.at[k]
        for i in range(CAP):
            row = masks[0:1, :] * flags[i][0]
            for p in range(1, held):
                row = row + masks[p : p + 1, :] * flags[i][p]
            meta[i : i + 1, :] = row
            for j in range(2):
                at = (1 + j) * CAP + i
                meta[at : at + 1, :] = jnp.full((1, edge), slot_ids[i][j], jnp.int32)
        meta[3 * CAP :, :] = jnp.zeros((meta.shape[0] - 3 * CAP, edge), jnp.int32)
    local[1].wait()
    for k in range(n_strat):
        flags, _ = plan[k]
        slots = recv_vals.at[own] if k == own else send_vals.at[k]
        for i in range(CAP):
            value = None
            for p in range(held):
                weight = jnp.full((edge, edge), flags[i][p].astype(jnp.float32)).astype(tiles.dtype)
                term = tiles[p] * weight
                value = term if value is None else value + term
            for h in range(phases):
                slots[h, i] = value[first_row(h) : first_row(h) + part]

    m_copies, v_copies = [], []
    for k in range(peers):
        dest, slot = other(k, me_s)
        m_copies.append(
            remote(send_meta.at[k], recv_meta.at[slot], m_send.at[k], m_recv.at[slot], strat=dest)
        )
        v_copies.append(
            [
                remote(
                    send_vals.at[k, h], recv_vals.at[slot, h], v_send.at[k, h], v_recv.at[slot, h],
                    strat=dest,
                )
                for h in range(phases)
            ]
        )
    @pl.when(side == 1)
    def _():
        pl.semaphore_wait(ready, 1)

    local[2].wait()

    @pl.when(chip > 0)
    def _():
        for e in range(2):
            u_copies[e].start()

    for k in range(peers):
        pl.when(k < me_s)(m_copies[k].start)

    @pl.when(me_s > 0)
    def _():
        for copy in v_copies[0]:
            copy.start()

    @pl.when(side == 1)
    def _():
        pl.semaphore_wait(barrier, n_rep - 1)
        signal(ready, rep=partner)

    @pl.when(side == 0)
    def _():
        pl.semaphore_wait(ready, 1)

    @pl.when(chip == 0)
    def _():
        for e in range(2):
            u_copies[e].start()

    for copy in u_copies[2:]:
        copy.start()

    for k in list(range(1, peers))[::-1]:
        @pl.when(k < me_s)
        def _():
            for copy in v_copies[k]:
                copy.start()

    for k in range(peers):
        @pl.when(k == me_s)
        def _():
            pl.semaphore_wait(strat_in.at[k + 1], 1)
            m_copies[k].start()
            v_copies[k][0].start()

    for k in range(peers):
        @pl.when(k > me_s)
        def _():
            pl.semaphore_wait(strat_in.at[k + 1], 1)
            m_copies[k].start()
            v_copies[k][0].start()

    for h in range(1, phases):
        for k in range(peers)[::-1]:
            @pl.when(k >= me_s)
            def _():
                v_copies[k][h].start()

    order = [own] + list(range(peers))

    def m_at(slot):
        return remote(
            send_meta.at[slot], recv_meta.at[slot], m_send.at[slot], m_recv.at[slot],
            strat=other(slot, me_s)[0],
        )

    def v_at(slot, h):
        return remote(
            send_vals.at[slot, h], recv_vals.at[slot, h], v_send.at[slot, h], v_recv.at[slot, h],
            strat=other(slot, me_s)[0],
        )

    def u_at(slot):
        return remote(
            own_rows, own_rows, u_send.at[slot], u_recv.at[slot], rep=partner
        )

    for k in range(peers):
        m_at(k).wait_recv()
    local[3].wait()
    def flags_of(r):
        meta = recv_meta[r].astype(jnp.float32)
        in_row, in_col = [], []
        for k in range(CAP):
            row_id, col_id = (meta[(1 + i) * CAP + k : (1 + i) * CAP + k + 1, :] for i in range(2))
            in_row.append([jnp.where(row_id == b, 1.0, 0.0) for b in range(n_row)])
            in_col.append([jnp.where(col_id == c, 1.0, 0.0) for c in range(n_col)])
        return meta, in_row, in_col

    for r in order:
        meta, _, in_col = flags_of(r)
        keep = meta.T
        for k in range(CAP):
            col_picks[r, k * edge : (k + 1) * edge, :] = pick(col_all, in_col[k])
            keeps[r, k] = jnp.broadcast_to(keep[:, k : k + 1], (edge, edge))

    for i in range(n_rep - 1):
        u_at(i).wait_recv()

    for r in order:
        _, in_row, _ = flags_of(r)
        for k in range(CAP):
            row_pick = pick(row_all, in_row[k])
            row_picks[r, k * edge : (k + 1) * edge, :] = row_pick
            predictions[r, k] = lax.dot_general(
                row_pick, col_picks[r, k * edge : (k + 1) * edge, :], (((1,), (1,)), ((), ())),
                preferred_element_type=jnp.float32,
            )

    def masked(error, flag):
        return error * jnp.broadcast_to(flag, error.shape).astype(error.dtype)

    def add_columns():
        total = None
        for r in order:
            _, _, in_col = flags_of(r)
            left = jnp.concatenate(
                [
                    jnp.concatenate(
                        [
                            masked(all_errors[r, k * edge : (k + 1) * edge, :], in_col[k][c])
                            for c in range(n_col)
                        ],
                        axis=1,
                    )
                    for k in range(CAP)
                ],
                axis=0,
            )
            term = lax.dot_general(
                left, row_picks[r], (((0,), (0,)), ((), ())),
                preferred_element_type=jnp.float32,
            )
            total = term if total is None else total + term
        col_out[...] = total * grad_scale

    d_copies, p_copies = [], []
    for h in range(phases):
        for at in range(0, n_strat, GROUP):
            group = order[at : at + GROUP]
            for r in group:
                if r != own:
                    v_at(r, h).wait_recv()
            lefts = []
            for r in group:
                _, row_same, _ = flags_of(r)
                errors = []
                for k in range(CAP):
                    here = slice(first_row(h), first_row(h) + part)
                    error = keeps[r, k, here, :] * (
                        predictions[r, k, here, :] - recv_vals[r, h, k].astype(jnp.float32)
                    )
                    error = error.astype(jnp.bfloat16)
                    errors.append(error)
                    first = k * edge + first_row(h)
                    all_errors[r, first : first + part, :] = error
                lefts.append(
                    jnp.concatenate(
                        [
                            jnp.concatenate(
                                [masked(errors[k], row_same[k][b]) for k in range(CAP)],
                                axis=1,
                            )
                            for b in range(n_row)
                        ],
                        axis=0,
                    )
                )
            term = jnp.dot(
                jnp.concatenate(lefts, axis=1),
                jnp.concatenate([col_picks[r] for r in group], axis=0),
                preferred_element_type=jnp.float32,
            )
            if at:
                term = row_acc[h] + term
            row_acc[h] = term
            if group[-1] == order[-1]:
                row_send[h] = term.astype(row_send.dtype)

        turn = h // 2
        within = pl.ds(turn * piece, piece)
        for k in range(pairs - 1):
            for e in [lax.rem(side + h, 2)] if phases > 1 else range(2):
                peer, slot = far_peer(k, e)
                start = peer // 2 * piece if phases > 1 else peer * piece
                i = len(d_copies)
                copy = remote(
                    row_send.at[h, pl.ds(pl.multiple_of(start, piece), piece)],
                    land_far.at[slot, within], d_send.at[i], d_recv.at[slot, turn], rep=peer,
                )
                copy.start()
                d_copies.append(copy)
        if phases == 1 or h % 2:
            start = chip * piece if phases > 1 else partner * piece
            which = 2 * turn + 1 - side if phases > 1 else 0
            p_copies.append(
                remote(
                    row_acc.at[which, pl.ds(pl.multiple_of(start, piece), piece)],
                    land_pair.at[within], p_send.at[turn], p_recv.at[turn], rep=partner,
                )
            )
        if phases == 1:
            p_copies[turn].start()
        elif h % 2:
            pl.when(side == 0)(p_copies[turn].start)
        else:
            pl.when(side == 1)(
                remote(
                    row_acc.at[h, pl.ds(pl.multiple_of(chip * piece, piece), piece)],
                    land_pair.at[within], p_send.at[turn], p_recv.at[turn], rep=partner,
                ).start
            )
    add_columns()
    for turn in range(turns):
        within = pl.ds(turn * piece, piece)
        p_copies[turn].wait_recv()
        which, start = (2 * turn + side, chip * piece) if phases > 1 else (0, me_q * piece)
        mine = row_acc[which, pl.ds(pl.multiple_of(start, piece), piece), :] + land_pair[within, :]
        for i in range(len(far)):
            remote(
                row_send.at[0, pl.ds(0, piece)], land_far.at[i, within], d_send.at[i],
                d_recv.at[i, turn], rep=partner,
            ).wait_recv()
            mine = mine + land_far[i, within, :].astype(jnp.float32)
        row_out[within, :] = mine * grad_scale

    for copy in u_copies + m_copies + sum(v_copies, []) + d_copies + p_copies:
        copy.wait_send()


def finish(row_in, col_in, row_out, col_out, sems):
    copies = [
        pltpu.make_async_copy(col_in, col_out, sems.at[0]),
        pltpu.make_async_copy(row_in, row_out, sems.at[1]),
    ]
    for copy in copies:
        copy.start()
    for copy in copies:
        copy.wait()


def on_device(
    ratings, row_mask, tile_owner, tile_row, tile_col, tile_count, row_factors, col_factors
):
    n_strat, n_rep = lax.axis_size("strat"), lax.axis_size("rep")
    edge = ratings.shape[1]
    rows, width = row_factors.shape
    cols = col_factors.shape[0]
    meta_rows = 8
    phases = 1
    if edge == 2 * rows and rows % (16 * TURNS) == 0:
        phases = 2 * TURNS
    turns = max(1, phases // 2)
    tile_count = tile_count.reshape(1, 1)
    hbm = pl.BlockSpec(memory_space=pltpu.HBM)
    vmem = pl.BlockSpec(memory_space=pltpu.VMEM)
    dma = pltpu.SemaphoreType.DMA
    row_grad, col_grad = pl.pallas_call(
        functools.partial(kernel, n_strat, n_rep),
        out_shape=(
            pltpu.VMEM((rows, width), jnp.float32),
            pltpu.VMEM((cols, width), jnp.float32),
        ),
        in_specs=[hbm] * 8,
        out_specs=(vmem, vmem),
        scratch_shapes=[
            pltpu.SMEM(tile_row.shape, jnp.int32),
            pltpu.SMEM(tile_row.shape, jnp.int32),
            pltpu.SMEM(tile_col.shape, jnp.int32),
            pltpu.SMEM(tile_count.shape, jnp.int32),
            pltpu.VMEM(ratings.shape, ratings.dtype),
            pltpu.VMEM(row_mask.shape, jnp.int32),
            pltpu.VMEM((n_rep * rows, width), row_factors.dtype),
            pltpu.VMEM((cols, width), col_factors.dtype),
            pltpu.VMEM((n_strat - 1, phases, CAP, edge // phases, edge), ratings.dtype),
            pltpu.VMEM((n_strat - 1, meta_rows, edge), jnp.int32),
            pltpu.VMEM((n_strat, phases, CAP, edge // phases, edge), ratings.dtype),
            pltpu.VMEM((n_strat, meta_rows, edge), jnp.int32),
            pltpu.VMEM((phases, n_rep * rows // phases, width), jnp.float32),
            pltpu.VMEM((phases, n_rep * rows // phases, width), jnp.bfloat16),
            pltpu.VMEM((n_strat, CAP * edge, edge), jnp.bfloat16),
            pltpu.VMEM((n_strat, CAP * edge, width), jnp.bfloat16),
            pltpu.VMEM((rows, width), jnp.float32),
            pltpu.VMEM((n_rep - 2, rows, width), jnp.bfloat16),
            pltpu.VMEM((n_strat, CAP, edge, edge), jnp.float32),
            pltpu.VMEM((n_strat, CAP, edge, edge), jnp.float32),
            pltpu.VMEM((n_strat, CAP * edge, width), jnp.bfloat16),
            dma((4,)),
            dma((4,)),
            dma((n_rep - 1,)),
            dma((n_rep - 1,)),
            dma((n_strat - 1, phases)),
            dma((n_strat - 1, phases)),
            dma((n_strat - 1,)),
            dma((n_strat - 1,)),
            dma((turns,)),
            dma((turns,)),
            dma((turns * (n_rep - 2),)),
            dma((n_rep - 2, turns)),
            pltpu.SemaphoreType.REGULAR,
            pltpu.SemaphoreType.REGULAR((n_strat,)),
        ],
        compiler_params=pltpu.CompilerParams(
            collective_id=0, has_side_effects=True
        ),
        name="gradient_pass",
    )(tile_owner.reshape(-1), tile_row, tile_col, tile_count, ratings, row_mask, row_factors, col_factors)
    row_grad, col_grad = (
        pltpu.with_memory_space_constraint(x, pltpu.VMEM) for x in (row_grad, col_grad)
    )
    anywhere = pl.BlockSpec(memory_space=pl.ANY)
    return pl.pallas_call(
        finish,
        out_shape=(
            jax.ShapeDtypeStruct((rows, width), jnp.float32),
            jax.ShapeDtypeStruct((cols, width), jnp.float32),
        ),
        in_specs=[anywhere] * 2,
        out_specs=(anywhere,) * 2,
        scratch_shapes=[dma((2,))],
        name="finish",
    )(row_grad, col_grad)


def solution(mesh):
    return jax.shard_map(
        on_device,
        mesh=mesh,
        in_specs=(
            P(("strat", "rep"), None, None),
            P(("strat", "rep"), None),
            P(("strat", "rep"), None),
            P(("strat", "rep")),
            P(("strat", "rep")),
            P(("strat", "rep")),
            P(("strat", "rep"), None),
            P(("strat", "rep"), None),
        ),
        out_specs=(P(("strat", "rep"), None), P(("strat", "rep"), None)),
        check_vma=False,
    )
```

```python
import functools

import jax
import jax.numpy as jnp
from jax import lax
from jax.experimental import pallas as pl
from jax.experimental.pallas import tpu as pltpu
from jax.sharding import PartitionSpec as P

CAP = 2
GROUPS = (4, 2)
TURNS = 1


grad_scale = 0.0625
MESH = pl.DeviceIdType.MESH


def remote(src, dst, send_sem, recv_sem, **where):
    return pltpu.make_async_remote_copy(
        src_ref=src,
        dst_ref=dst,
        send_sem=send_sem,
        recv_sem=recv_sem,
        device_id=where,
        device_id_type=MESH,
    )


def kernel(
    n_strat, n_rep,
    owner_in, tile_row_in, tile_col_in, count_in, ratings, row_mask, row_factors, col_factors,
    row_out, col_out,
    owner, tile_row, tile_col, count,
    tiles, masks, row_all, col_all, send_vals, send_meta, recv_vals, recv_meta,
    row_acc, row_send, all_errors, row_picks, land_pair, land_far,
    predictions, keeps, col_picks,
    small_sem, local_sem, u_send, u_recv, v_send, v_recv, m_send, m_recv,
    p_send, p_recv, d_send, d_recv, ready, strat_in,
):
    held, edge = tiles.shape[0], tiles.shape[1]
    rows = row_factors.shape[0]
    n_row, n_col = row_all.shape[0] // edge, col_all.shape[0] // edge
    me_s, me_q = lax.axis_index("strat"), lax.axis_index("rep")
    pairs = n_rep // 2
    chip, side = me_q // 2, lax.rem(me_q, 2)
    partner = 2 * chip + 1 - side
    peers, own = n_strat - 1, n_strat - 1
    phases, part = send_vals.shape[1], send_vals.shape[3]
    turns = max(1, phases // 2)
    piece = rows // turns

    def rows_of(index):
        return pl.ds(pl.multiple_of(index * rows, rows), rows)

    def first_row(h):
        return h % 2 * rows + h // 2 * part if phases > 1 else 0

    def other(k, me):
        past = jnp.where(k >= me, 1, 0)
        return k + past, me - 1 + past

    def pick(blocks, same):
        wide = blocks.shape[1] // edge
        chosen = None
        for b, flag in enumerate(same):
            flag = jnp.concatenate([flag] * wide, axis=1)
            weight = jnp.broadcast_to(flag, (edge, wide * edge)).astype(blocks.dtype)
            part = blocks[b * edge : (b + 1) * edge, :]
            chosen = part if chosen is None else jnp.where(weight > 0, part, chosen)
        return chosen

    local = [
        pltpu.make_async_copy(row_mask, masks, local_sem.at[0]),
        pltpu.make_async_copy(ratings, tiles, local_sem.at[1]),
        pltpu.make_async_copy(row_factors, row_all.at[rows_of(me_q)], local_sem.at[2]),
        pltpu.make_async_copy(col_factors, col_all, local_sem.at[3]),
    ]
    small = [
        pltpu.make_async_copy(source, target, small_sem.at[i])
        for i, (source, target) in enumerate(
            [(owner_in, owner), (tile_row_in, tile_row), (tile_col_in, tile_col), (count_in, count)]
        )
    ]
    barrier = pltpu.get_barrier_semaphore()

    def signal(semaphore, **where):
        pl.semaphore_signal(semaphore, inc=1, device_id=where, device_id_type=MESH)

    for k in range(pairs - 1):
        pair = other(k, chip)[0]
        signal(barrier, rep=2 * pair + 1)

        @pl.when(chip == 0)
        def _():
            signal(barrier, rep=2 * pair)

    signal(barrier, rep=partner)
    for k in range(peers):
        @pl.when(k >= me_s)
        def _():
            signal(barrier, strat=k + 1, rep=2 * chip)

    for copy in small + local[:2]:
        copy.start()

    for copy in local[2:]:
        copy.start()

    @pl.when(side == 0)
    def _():
        pl.semaphore_wait(barrier, 2 * me_s + jnp.where(chip == 0, 1, 3))
        signal(ready, rep=partner)
        for k in range(peers):
            @pl.when(k < me_s)
            def _():
                for e in range(2):
                    signal(strat_in.at[me_s], strat=k, rep=2 * chip + e)

    far = [(k, e) for k in range(pairs - 1) for e in range(2)]

    def far_peer(k, e):
        target, slot = other(k, chip)
        return 2 * target + lax.rem(side + e, 2), 2 * slot + e

    own_rows = row_all.at[rows_of(me_q)]
    u_copies = []
    for i, (k, e) in enumerate(far):
        peer, slot = far_peer(k, e)
        u_copies.append(
            remote(own_rows, own_rows, u_send.at[i], u_recv.at[slot], rep=peer)
        )
    u_copies.append(
        remote(
            own_rows, own_rows, u_send.at[len(far)], u_recv.at[len(far)], rep=partner,
        )
    )

    for copy in small:
        copy.wait()

    live = [p < count[0, 0] for p in range(held)]
    owners = [owner[p] for p in range(held)]
    plan = []
    for k in range(n_strat):
        dest = me_s if k == own else other(k, me_s)[0]
        seen = jnp.int32(0)
        flags = [[] for _ in range(CAP)]
        slot_ids = [[jnp.int32(0), jnp.int32(0)] for _ in range(CAP)]
        for p in range(held):
            here = jnp.where(jnp.logical_and(live[p], owners[p] == dest), 1, 0)
            for i in range(CAP):
                flag = jnp.where(seen == i, here, 0)
                flags[i].append(flag)
                slot_ids[i][0] += flag * tile_row[p]
                slot_ids[i][1] += flag * tile_col[p]
            seen = seen + here
        plan.append((flags, slot_ids))

    local[0].wait()
    for k in range(n_strat):
        flags, slot_ids = plan[k]
        meta = recv_meta.at[own] if k == own else send_meta.at[k]
        for i in range(CAP):
            row = masks[0:1, :] * flags[i][0]
            for p in range(1, held):
                row = row + masks[p : p + 1, :] * flags[i][p]
            meta[i : i + 1, :] = row
            for j in range(2):
                at = (1 + j) * CAP + i
                meta[at : at + 1, :] = jnp.full((1, edge), slot_ids[i][j], jnp.int32)
        meta[3 * CAP :, :] = jnp.zeros((meta.shape[0] - 3 * CAP, edge), jnp.int32)
    local[1].wait()
    for k in range(n_strat):
        flags, _ = plan[k]
        slots = recv_vals.at[own] if k == own else send_vals.at[k]
        for i in range(CAP):
            value = None
            for p in range(held):
                weight = jnp.full((edge, edge), flags[i][p].astype(jnp.float32)).astype(tiles.dtype)
                term = tiles[p] * weight
                value = term if value is None else value + term
            for h in range(phases):
                slots[h, i] = value[first_row(h) : first_row(h) + part]

    m_copies, v_copies = [], []
    for k in range(peers):
        dest, slot = other(k, me_s)
        m_copies.append(
            remote(send_meta.at[k], recv_meta.at[slot], m_send.at[k], m_recv.at[slot], strat=dest)
        )
        v_copies.append(
            [
                remote(
                    send_vals.at[k, h], recv_vals.at[slot, h], v_send.at[k, h], v_recv.at[slot, h],
                    strat=dest,
                )
                for h in range(phases)
            ]
        )
    @pl.when(side == 1)
    def _():
        pl.semaphore_wait(ready, 1)

    local[2].wait()

    @pl.when(chip > 0)
    def _():
        for e in range(2):
            u_copies[e].start()

    for k in range(peers):
        pl.when(k < me_s)(m_copies[k].start)

    @pl.when(me_s > 0)
    def _():
        for copy in v_copies[0]:
            copy.start()

    @pl.when(side == 1)
    def _():
        pl.semaphore_wait(barrier, n_rep - 1)
        signal(ready, rep=partner)

    @pl.when(side == 0)
    def _():
        pl.semaphore_wait(ready, 1)

    @pl.when(chip == 0)
    def _():
        for e in range(2):
            u_copies[e].start()

    for copy in u_copies[2:]:
        copy.start()

    for k in list(range(1, peers))[::-1]:
        @pl.when(k < me_s)
        def _():
            for copy in v_copies[k]:
                copy.start()

    for k in range(peers):
        @pl.when(k == me_s)
        def _():
            pl.semaphore_wait(strat_in.at[k + 1], 1)
            m_copies[k].start()
            v_copies[k][0].start()

    for k in range(peers):
        @pl.when(k > me_s)
        def _():
            pl.semaphore_wait(strat_in.at[k + 1], 1)
            m_copies[k].start()
            v_copies[k][0].start()

    for h in range(1, phases):
        for k in range(peers)[::-1]:
            @pl.when(k >= me_s)
            def _():
                v_copies[k][h].start()

    order = [own] + list(range(peers))

    def m_at(slot):
        return remote(
            send_meta.at[slot], recv_meta.at[slot], m_send.at[slot], m_recv.at[slot],
            strat=other(slot, me_s)[0],
        )

    def v_at(slot, h):
        return remote(
            send_vals.at[slot, h], recv_vals.at[slot, h], v_send.at[slot, h], v_recv.at[slot, h],
            strat=other(slot, me_s)[0],
        )

    def u_at(slot):
        return remote(
            own_rows, own_rows, u_send.at[slot], u_recv.at[slot], rep=partner
        )

    for k in range(peers):
        m_at(k).wait_recv()
    local[3].wait()
    def flags_of(r):
        meta = recv_meta[r].astype(jnp.float32)
        in_row, in_col = [], []
        for k in range(CAP):
            row_id, col_id = (meta[(1 + i) * CAP + k : (1 + i) * CAP + k + 1, :] for i in range(2))
            in_row.append([jnp.where(row_id == b, 1.0, 0.0) for b in range(n_row)])
            in_col.append([jnp.where(col_id == c, 1.0, 0.0) for c in range(n_col)])
        return meta, in_row, in_col

    for r in order:
        meta, _, in_col = flags_of(r)
        keep = meta.T
        for k in range(CAP):
            col_picks[r, k * edge : (k + 1) * edge, :] = pick(col_all, in_col[k])
            keeps[r, k] = jnp.broadcast_to(keep[:, k : k + 1], (edge, edge))

    for i in range(n_rep - 1):
        u_at(i).wait_recv()

    for r in order:
        _, in_row, _ = flags_of(r)
        for k in range(CAP):
            row_pick = pick(row_all, in_row[k])
            row_picks[r, k * edge : (k + 1) * edge, :] = row_pick
            predictions[r, k] = lax.dot_general(
                row_pick, col_picks[r, k * edge : (k + 1) * edge, :], (((1,), (1,)), ((), ())),
                preferred_element_type=jnp.float32,
            )

    def masked(error, flag):
        return error * jnp.broadcast_to(flag, error.shape).astype(error.dtype)

    def add_columns():
        total = None
        for r in order:
            _, _, in_col = flags_of(r)
            left = jnp.concatenate(
                [
                    jnp.concatenate(
                        [
                            masked(all_errors[r, k * edge : (k + 1) * edge, :], in_col[k][c])
                            for c in range(n_col)
                        ],
                        axis=1,
                    )
                    for k in range(CAP)
                ],
                axis=0,
            )
            term = lax.dot_general(
                left, row_picks[r], (((0,), (0,)), ((), ())),
                preferred_element_type=jnp.float32,
            )
            total = term if total is None else total + term
        col_out[...] = total * grad_scale

    d_copies, p_copies = [], []
    for h in range(phases):
        size = GROUPS[h]
        for at in range(0, n_strat, size):
            group = order[at : at + size]
            for r in group:
                if r != own:
                    v_at(r, h).wait_recv()
            lefts = []
            for r in group:
                _, row_same, _ = flags_of(r)
                errors = []
                for k in range(CAP):
                    here = slice(first_row(h), first_row(h) + part)
                    error = keeps[r, k, here, :] * (
                        predictions[r, k, here, :] - recv_vals[r, h, k].astype(jnp.float32)
                    )
                    error = error.astype(jnp.bfloat16)
                    errors.append(error)
                    first = k * edge + first_row(h)
                    all_errors[r, first : first + part, :] = error
                lefts.append(
                    jnp.concatenate(
                        [
                            jnp.concatenate(
                                [masked(errors[k], row_same[k][b]) for k in range(CAP)],
                                axis=1,
                            )
                            for b in range(n_row)
                        ],
                        axis=0,
                    )
                )
            term = jnp.dot(
                jnp.concatenate(lefts, axis=1),
                jnp.concatenate([col_picks[r] for r in group], axis=0),
                preferred_element_type=jnp.float32,
            )
            if at:
                term = row_acc[h] + term
            row_acc[h] = term
            if group[-1] == order[-1]:
                row_send[h] = term.astype(row_send.dtype)

        turn = h // 2
        within = pl.ds(turn * piece, piece)
        for k in range(pairs - 1):
            for e in [lax.rem(side + h, 2)] if phases > 1 else range(2):
                peer, slot = far_peer(k, e)
                start = peer // 2 * piece if phases > 1 else peer * piece
                i = len(d_copies)
                copy = remote(
                    row_send.at[h, pl.ds(pl.multiple_of(start, piece), piece)],
                    land_far.at[slot, within], d_send.at[i], d_recv.at[slot, turn], rep=peer,
                )
                copy.start()
                d_copies.append(copy)
        if phases == 1 or h % 2:
            start = chip * piece if phases > 1 else partner * piece
            which = 2 * turn + 1 - side if phases > 1 else 0
            p_copies.append(
                remote(
                    row_acc.at[which, pl.ds(pl.multiple_of(start, piece), piece)],
                    land_pair.at[within], p_send.at[turn], p_recv.at[turn], rep=partner,
                )
            )
        if phases == 1:
            p_copies[turn].start()
        elif h % 2:
            pl.when(side == 0)(p_copies[turn].start)
        else:
            pl.when(side == 1)(
                remote(
                    row_acc.at[h, pl.ds(pl.multiple_of(chip * piece, piece), piece)],
                    land_pair.at[within], p_send.at[turn], p_recv.at[turn], rep=partner,
                ).start
            )
    add_columns()
    for turn in range(turns):
        within = pl.ds(turn * piece, piece)
        p_copies[turn].wait_recv()
        which, start = (2 * turn + side, chip * piece) if phases > 1 else (0, me_q * piece)
        mine = row_acc[which, pl.ds(pl.multiple_of(start, piece), piece), :] + land_pair[within, :]
        for i in range(len(far)):
            remote(
                row_send.at[0, pl.ds(0, piece)], land_far.at[i, within], d_send.at[i],
                d_recv.at[i, turn], rep=partner,
            ).wait_recv()
            mine = mine + land_far[i, within, :].astype(jnp.float32)
        row_out[within, :] = mine * grad_scale

    for copy in u_copies + m_copies + sum(v_copies, []) + d_copies + p_copies:
        copy.wait_send()


def finish(row_in, col_in, row_out, col_out, sems):
    copies = [
        pltpu.make_async_copy(col_in, col_out, sems.at[0]),
        pltpu.make_async_copy(row_in, row_out, sems.at[1]),
    ]
    for copy in copies:
        copy.start()
    for copy in copies:
        copy.wait()


def on_device(
    ratings, row_mask, tile_owner, tile_row, tile_col, tile_count, row_factors, col_factors
):
    n_strat, n_rep = lax.axis_size("strat"), lax.axis_size("rep")
    edge = ratings.shape[1]
    rows, width = row_factors.shape
    cols = col_factors.shape[0]
    meta_rows = 8
    phases = 1
    if edge == 2 * rows and rows % (16 * TURNS) == 0:
        phases = 2 * TURNS
    turns = max(1, phases // 2)
    tile_count = tile_count.reshape(1, 1)
    hbm = pl.BlockSpec(memory_space=pltpu.HBM)
    vmem = pl.BlockSpec(memory_space=pltpu.VMEM)
    dma = pltpu.SemaphoreType.DMA
    row_grad, col_grad = pl.pallas_call(
        functools.partial(kernel, n_strat, n_rep),
        out_shape=(
            pltpu.VMEM((rows, width), jnp.float32),
            pltpu.VMEM((cols, width), jnp.float32),
        ),
        in_specs=[hbm] * 8,
        out_specs=(vmem, vmem),
        scratch_shapes=[
            pltpu.SMEM(tile_row.shape, jnp.int32),
            pltpu.SMEM(tile_row.shape, jnp.int32),
            pltpu.SMEM(tile_col.shape, jnp.int32),
            pltpu.SMEM(tile_count.shape, jnp.int32),
            pltpu.VMEM(ratings.shape, ratings.dtype),
            pltpu.VMEM(row_mask.shape, jnp.int32),
            pltpu.VMEM((n_rep * rows, width), row_factors.dtype),
            pltpu.VMEM((cols, width), col_factors.dtype),
            pltpu.VMEM((n_strat - 1, phases, CAP, edge // phases, edge), ratings.dtype),
            pltpu.VMEM((n_strat - 1, meta_rows, edge), jnp.int32),
            pltpu.VMEM((n_strat, phases, CAP, edge // phases, edge), ratings.dtype),
            pltpu.VMEM((n_strat, meta_rows, edge), jnp.int32),
            pltpu.VMEM((phases, n_rep * rows // phases, width), jnp.float32),
            pltpu.VMEM((phases, n_rep * rows // phases, width), jnp.bfloat16),
            pltpu.VMEM((n_strat, CAP * edge, edge), jnp.bfloat16),
            pltpu.VMEM((n_strat, CAP * edge, width), jnp.bfloat16),
            pltpu.VMEM((rows, width), jnp.float32),
            pltpu.VMEM((n_rep - 2, rows, width), jnp.bfloat16),
            pltpu.VMEM((n_strat, CAP, edge, edge), jnp.float32),
            pltpu.VMEM((n_strat, CAP, edge, edge), jnp.float32),
            pltpu.VMEM((n_strat, CAP * edge, width), jnp.bfloat16),
            dma((4,)),
            dma((4,)),
            dma((n_rep - 1,)),
            dma((n_rep - 1,)),
            dma((n_strat - 1, phases)),
            dma((n_strat - 1, phases)),
            dma((n_strat - 1,)),
            dma((n_strat - 1,)),
            dma((turns,)),
            dma((turns,)),
            dma((turns * (n_rep - 2),)),
            dma((n_rep - 2, turns)),
            pltpu.SemaphoreType.REGULAR,
            pltpu.SemaphoreType.REGULAR((n_strat,)),
        ],
        compiler_params=pltpu.CompilerParams(
            collective_id=0, has_side_effects=True
        ),
        name="gradient_pass",
    )(tile_owner.reshape(-1), tile_row, tile_col, tile_count, ratings, row_mask, row_factors, col_factors)
    row_grad, col_grad = (
        pltpu.with_memory_space_constraint(x, pltpu.VMEM) for x in (row_grad, col_grad)
    )
    anywhere = pl.BlockSpec(memory_space=pl.ANY)
    return pl.pallas_call(
        finish,
        out_shape=(
            jax.ShapeDtypeStruct((rows, width), jnp.float32),
            jax.ShapeDtypeStruct((cols, width), jnp.float32),
        ),
        in_specs=[anywhere] * 2,
        out_specs=(anywhere,) * 2,
        scratch_shapes=[dma((2,))],
        name="finish",
    )(row_grad, col_grad)


def solution(mesh):
    return jax.shard_map(
        on_device,
        mesh=mesh,
        in_specs=(
            P(("strat", "rep"), None, None),
            P(("strat", "rep"), None),
            P(("strat", "rep"), None),
            P(("strat", "rep")),
            P(("strat", "rep")),
            P(("strat", "rep")),
            P(("strat", "rep"), None),
            P(("strat", "rep"), None),
        ),
        out_specs=(P(("strat", "rep"), None), P(("strat", "rep"), None)),
        check_vma=False,
    )
```

```python
import functools

import jax
import jax.numpy as jnp
from jax import lax
from jax.experimental import pallas as pl
from jax.experimental.pallas import tpu as pltpu
from jax.sharding import PartitionSpec as P

CAP = 2
GROUPS = (4, 2)
TURNS = 1


grad_scale = 0.0625
MESH = pl.DeviceIdType.MESH


def remote(src, dst, send_sem, recv_sem, **where):
    return pltpu.make_async_remote_copy(
        src_ref=src,
        dst_ref=dst,
        send_sem=send_sem,
        recv_sem=recv_sem,
        device_id=where,
        device_id_type=MESH,
    )


def kernel(
    n_strat, n_rep,
    owner_in, tile_row_in, tile_col_in, count_in, ratings, row_mask, row_factors, col_factors,
    row_out, col_out,
    owner, tile_row, tile_col, count,
    tiles, masks, row_all, col_all, send_vals, send_meta, recv_vals, recv_meta,
    row_acc, row_send, all_errors, row_picks, land_pair, land_far,
    predictions, keeps, col_picks,
    small_sem, local_sem, u_send, u_recv, v_send, v_recv, m_send, m_recv,
    p_send, p_recv, d_send, d_recv, ready, strat_in,
):
    held, edge = tiles.shape[0], tiles.shape[1]
    rows = row_factors.shape[0]
    n_row, n_col = row_all.shape[0] // edge, col_all.shape[0] // edge
    me_s, me_q = lax.axis_index("strat"), lax.axis_index("rep")
    pairs = n_rep // 2
    chip, side = me_q // 2, lax.rem(me_q, 2)
    partner = 2 * chip + 1 - side
    peers, own = n_strat - 1, n_strat - 1
    phases, part = send_vals.shape[1], send_vals.shape[3]
    turns = max(1, phases // 2)
    piece = rows // turns

    def rows_of(index):
        return pl.ds(pl.multiple_of(index * rows, rows), rows)

    def first_row(h):
        return h % 2 * rows + h // 2 * part if phases > 1 else 0

    def other(k, me):
        past = jnp.where(k >= me, 1, 0)
        return k + past, me - 1 + past

    def pick(blocks, same):
        wide = blocks.shape[1] // edge
        chosen = None
        for b, flag in enumerate(same):
            flag = jnp.concatenate([flag] * wide, axis=1)
            weight = jnp.broadcast_to(flag, (edge, wide * edge)).astype(blocks.dtype)
            part = blocks[b * edge : (b + 1) * edge, :]
            chosen = part if chosen is None else jnp.where(weight > 0, part, chosen)
        return chosen

    local = [
        pltpu.make_async_copy(row_mask, masks, local_sem.at[0]),
        pltpu.make_async_copy(ratings, tiles, local_sem.at[1]),
        pltpu.make_async_copy(row_factors, row_all.at[rows_of(me_q)], local_sem.at[2]),
        pltpu.make_async_copy(col_factors, col_all, local_sem.at[3]),
    ]
    small = [
        pltpu.make_async_copy(source, target, small_sem.at[i])
        for i, (source, target) in enumerate(
            [(owner_in, owner), (tile_row_in, tile_row), (tile_col_in, tile_col), (count_in, count)]
        )
    ]
    barrier = pltpu.get_barrier_semaphore()

    def signal(semaphore, **where):
        pl.semaphore_signal(semaphore, inc=1, device_id=where, device_id_type=MESH)

    for k in range(pairs - 1):
        pair = other(k, chip)[0]
        signal(barrier, rep=2 * pair + 1)

        @pl.when(chip == 0)
        def _():
            signal(barrier, rep=2 * pair)

    signal(barrier, rep=partner)
    for k in range(peers):
        @pl.when(k >= me_s)
        def _():
            signal(barrier, strat=k + 1, rep=2 * chip)

    for copy in small + local[1::-1] + [local[2]]:
        copy.start()

    local[3].start()

    @pl.when(side == 0)
    def _():
        pl.semaphore_wait(barrier, 2 * me_s + jnp.where(chip == 0, 1, 3))
        signal(ready, rep=partner)
        for k in range(peers):
            @pl.when(k < me_s)
            def _():
                for e in range(2):
                    signal(strat_in.at[me_s], strat=k, rep=2 * chip + e)

    far = [(k, e) for k in range(pairs - 1) for e in range(2)]

    def far_peer(k, e):
        target, slot = other(k, chip)
        return 2 * target + lax.rem(side + e, 2), 2 * slot + e

    own_rows = row_all.at[rows_of(me_q)]
    u_copies = []
    for i, (k, e) in enumerate(far):
        peer, slot = far_peer(k, e)
        u_copies.append(
            remote(own_rows, own_rows, u_send.at[i], u_recv.at[slot], rep=peer)
        )
    u_copies.append(
        remote(
            own_rows, own_rows, u_send.at[len(far)], u_recv.at[len(far)], rep=partner,
        )
    )

    for copy in small:
        copy.wait()

    live = [p < count[0, 0] for p in range(held)]
    owners = [owner[p] for p in range(held)]
    plan = []
    for k in range(n_strat):
        dest = me_s if k == own else other(k, me_s)[0]
        seen = jnp.int32(0)
        flags = [[] for _ in range(CAP)]
        slot_ids = [[jnp.int32(0), jnp.int32(0)] for _ in range(CAP)]
        for p in range(held):
            here = jnp.where(jnp.logical_and(live[p], owners[p] == dest), 1, 0)
            for i in range(CAP):
                flag = jnp.where(seen == i, here, 0)
                flags[i].append(flag)
                slot_ids[i][0] += flag * tile_row[p]
                slot_ids[i][1] += flag * tile_col[p]
            seen = seen + here
        plan.append((flags, slot_ids))

    local[0].wait()
    for k in range(n_strat):
        flags, slot_ids = plan[k]
        meta = recv_meta.at[own] if k == own else send_meta.at[k]
        for i in range(CAP):
            row = masks[0:1, :] * flags[i][0]
            for p in range(1, held):
                row = row + masks[p : p + 1, :] * flags[i][p]
            meta[i : i + 1, :] = row
            for j in range(2):
                at = (1 + j) * CAP + i
                meta[at : at + 1, :] = jnp.full((1, edge), slot_ids[i][j], jnp.int32)
        meta[3 * CAP :, :] = jnp.zeros((meta.shape[0] - 3 * CAP, edge), jnp.int32)
    local[1].wait()
    for k in range(n_strat):
        flags, _ = plan[k]
        slots = recv_vals.at[own] if k == own else send_vals.at[k]
        for i in range(CAP):
            value = None
            for p in range(held):
                weight = jnp.full((edge, edge), flags[i][p].astype(jnp.float32)).astype(tiles.dtype)
                term = tiles[p] * weight
                value = term if value is None else value + term
            for h in range(phases):
                slots[h, i] = value[first_row(h) : first_row(h) + part]

    m_copies, v_copies = [], []
    for k in range(peers):
        dest, slot = other(k, me_s)
        m_copies.append(
            remote(send_meta.at[k], recv_meta.at[slot], m_send.at[k], m_recv.at[slot], strat=dest)
        )
        v_copies.append(
            [
                remote(
                    send_vals.at[k, h], recv_vals.at[slot, h], v_send.at[k, h], v_recv.at[slot, h],
                    strat=dest,
                )
                for h in range(phases)
            ]
        )
    @pl.when(side == 1)
    def _():
        pl.semaphore_wait(ready, 1)

    local[2].wait()

    @pl.when(chip > 0)
    def _():
        for e in range(2):
            u_copies[e].start()

    for k in range(peers):
        pl.when(k < me_s)(m_copies[k].start)

    @pl.when(me_s > 0)
    def _():
        for copy in v_copies[0]:
            copy.start()

    @pl.when(side == 1)
    def _():
        pl.semaphore_wait(barrier, n_rep - 1)
        signal(ready, rep=partner)

    @pl.when(side == 0)
    def _():
        pl.semaphore_wait(ready, 1)

    @pl.when(chip == 0)
    def _():
        for e in range(2):
            u_copies[e].start()

    for copy in u_copies[2:]:
        copy.start()

    for k in list(range(1, peers))[::-1]:
        @pl.when(k < me_s)
        def _():
            for copy in v_copies[k]:
                copy.start()

    for k in range(peers):
        @pl.when(k == me_s)
        def _():
            pl.semaphore_wait(strat_in.at[k + 1], 1)
            m_copies[k].start()
            v_copies[k][0].start()

    for k in range(peers):
        @pl.when(k > me_s)
        def _():
            pl.semaphore_wait(strat_in.at[k + 1], 1)
            m_copies[k].start()
            v_copies[k][0].start()

    for h in range(1, phases):
        for k in range(peers)[::-1]:
            @pl.when(k >= me_s)
            def _():
                v_copies[k][h].start()

    order = [own] + list(range(peers))

    def m_at(slot):
        return remote(
            send_meta.at[slot], recv_meta.at[slot], m_send.at[slot], m_recv.at[slot],
            strat=other(slot, me_s)[0],
        )

    def v_at(slot, h):
        return remote(
            send_vals.at[slot, h], recv_vals.at[slot, h], v_send.at[slot, h], v_recv.at[slot, h],
            strat=other(slot, me_s)[0],
        )

    def u_at(slot):
        return remote(
            own_rows, own_rows, u_send.at[slot], u_recv.at[slot], rep=partner
        )

    for k in range(peers):
        m_at(k).wait_recv()
    local[3].wait()
    def flags_of(r):
        meta = recv_meta[r].astype(jnp.float32)
        in_row, in_col = [], []
        for k in range(CAP):
            row_id, col_id = (meta[(1 + i) * CAP + k : (1 + i) * CAP + k + 1, :] for i in range(2))
            in_row.append([jnp.where(row_id == b, 1.0, 0.0) for b in range(n_row)])
            in_col.append([jnp.where(col_id == c, 1.0, 0.0) for c in range(n_col)])
        return meta, in_row, in_col

    for r in order:
        meta, _, in_col = flags_of(r)
        keep = meta.T
        for k in range(CAP):
            col_picks[r, k * edge : (k + 1) * edge, :] = pick(col_all, in_col[k])
            keeps[r, k] = jnp.broadcast_to(keep[:, k : k + 1], (edge, edge))

    for i in range(n_rep - 1):
        u_at(i).wait_recv()

    for r in order:
        _, in_row, _ = flags_of(r)
        for k in range(CAP):
            row_pick = pick(row_all, in_row[k])
            row_picks[r, k * edge : (k + 1) * edge, :] = row_pick
            predictions[r, k] = lax.dot_general(
                row_pick, col_picks[r, k * edge : (k + 1) * edge, :], (((1,), (1,)), ((), ())),
                preferred_element_type=jnp.float32,
            )

    def masked(error, flag):
        return error * jnp.broadcast_to(flag, error.shape).astype(error.dtype)

    def add_columns():
        total = None
        for r in order:
            _, _, in_col = flags_of(r)
            left = jnp.concatenate(
                [
                    jnp.concatenate(
                        [
                            masked(all_errors[r, k * edge : (k + 1) * edge, :], in_col[k][c])
                            for c in range(n_col)
                        ],
                        axis=1,
                    )
                    for k in range(CAP)
                ],
                axis=0,
            )
            term = lax.dot_general(
                left, row_picks[r], (((0,), (0,)), ((), ())),
                preferred_element_type=jnp.float32,
            )
            total = term if total is None else total + term
        col_out[...] = total * grad_scale

    d_copies, p_copies = [], []
    for h in range(phases):
        size = GROUPS[h]
        for at in range(0, n_strat, size):
            group = order[at : at + size]
            for r in group:
                if r != own:
                    v_at(r, h).wait_recv()
            lefts = []
            for r in group:
                _, row_same, _ = flags_of(r)
                errors = []
                for k in range(CAP):
                    here = slice(first_row(h), first_row(h) + part)
                    error = keeps[r, k, here, :] * (
                        predictions[r, k, here, :] - recv_vals[r, h, k].astype(jnp.float32)
                    )
                    error = error.astype(jnp.bfloat16)
                    errors.append(error)
                    first = k * edge + first_row(h)
                    all_errors[r, first : first + part, :] = error
                lefts.append(
                    jnp.concatenate(
                        [
                            jnp.concatenate(
                                [masked(errors[k], row_same[k][b]) for k in range(CAP)],
                                axis=1,
                            )
                            for b in range(n_row)
                        ],
                        axis=0,
                    )
                )
            term = jnp.dot(
                jnp.concatenate(lefts, axis=1),
                jnp.concatenate([col_picks[r] for r in group], axis=0),
                preferred_element_type=jnp.float32,
            )
            if at:
                term = row_acc[h] + term
            row_acc[h] = term
            if group[-1] == order[-1]:
                row_send[h] = term.astype(row_send.dtype)

        turn = h // 2
        within = pl.ds(turn * piece, piece)
        for k in range(pairs - 1):
            for e in [lax.rem(side + h, 2)] if phases > 1 else range(2):
                peer, slot = far_peer(k, e)
                start = peer // 2 * piece if phases > 1 else peer * piece
                i = len(d_copies)
                copy = remote(
                    row_send.at[h, pl.ds(pl.multiple_of(start, piece), piece)],
                    land_far.at[slot, within], d_send.at[i], d_recv.at[slot, turn], rep=peer,
                )
                copy.start()
                d_copies.append(copy)
        if phases == 1 or h % 2:
            start = chip * piece if phases > 1 else partner * piece
            which = 2 * turn + 1 - side if phases > 1 else 0
            p_copies.append(
                remote(
                    row_acc.at[which, pl.ds(pl.multiple_of(start, piece), piece)],
                    land_pair.at[within], p_send.at[turn], p_recv.at[turn], rep=partner,
                )
            )
        if phases == 1:
            p_copies[turn].start()
        elif h % 2:
            pl.when(side == 0)(p_copies[turn].start)
        else:
            pl.when(side == 1)(
                remote(
                    row_acc.at[h, pl.ds(pl.multiple_of(chip * piece, piece), piece)],
                    land_pair.at[within], p_send.at[turn], p_recv.at[turn], rep=partner,
                ).start
            )
    add_columns()
    for turn in range(turns):
        within = pl.ds(turn * piece, piece)
        p_copies[turn].wait_recv()
        which, start = (2 * turn + side, chip * piece) if phases > 1 else (0, me_q * piece)
        mine = row_acc[which, pl.ds(pl.multiple_of(start, piece), piece), :] + land_pair[within, :]
        for i in range(len(far)):
            remote(
                row_send.at[0, pl.ds(0, piece)], land_far.at[i, within], d_send.at[i],
                d_recv.at[i, turn], rep=partner,
            ).wait_recv()
            mine = mine + land_far[i, within, :].astype(jnp.float32)
        row_out[within, :] = mine * grad_scale

    for copy in u_copies + m_copies + sum(v_copies, []) + d_copies + p_copies:
        copy.wait_send()


def finish(row_in, col_in, row_out, col_out, sems):
    copies = [
        pltpu.make_async_copy(col_in, col_out, sems.at[0]),
        pltpu.make_async_copy(row_in, row_out, sems.at[1]),
    ]
    for copy in copies:
        copy.start()
    for copy in copies:
        copy.wait()


def on_device(
    ratings, row_mask, tile_owner, tile_row, tile_col, tile_count, row_factors, col_factors
):
    n_strat, n_rep = lax.axis_size("strat"), lax.axis_size("rep")
    edge = ratings.shape[1]
    rows, width = row_factors.shape
    cols = col_factors.shape[0]
    meta_rows = 8
    phases = 1
    if edge == 2 * rows and rows % (16 * TURNS) == 0:
        phases = 2 * TURNS
    turns = max(1, phases // 2)
    tile_count = tile_count.reshape(1, 1)
    hbm = pl.BlockSpec(memory_space=pltpu.HBM)
    vmem = pl.BlockSpec(memory_space=pltpu.VMEM)
    dma = pltpu.SemaphoreType.DMA
    row_grad, col_grad = pl.pallas_call(
        functools.partial(kernel, n_strat, n_rep),
        out_shape=(
            pltpu.VMEM((rows, width), jnp.float32),
            pltpu.VMEM((cols, width), jnp.float32),
        ),
        in_specs=[hbm] * 8,
        out_specs=(vmem, vmem),
        scratch_shapes=[
            pltpu.SMEM(tile_row.shape, jnp.int32),
            pltpu.SMEM(tile_row.shape, jnp.int32),
            pltpu.SMEM(tile_col.shape, jnp.int32),
            pltpu.SMEM(tile_count.shape, jnp.int32),
            pltpu.VMEM(ratings.shape, ratings.dtype),
            pltpu.VMEM(row_mask.shape, jnp.int32),
            pltpu.VMEM((n_rep * rows, width), row_factors.dtype),
            pltpu.VMEM((cols, width), col_factors.dtype),
            pltpu.VMEM((n_strat - 1, phases, CAP, edge // phases, edge), ratings.dtype),
            pltpu.VMEM((n_strat - 1, meta_rows, edge), jnp.int32),
            pltpu.VMEM((n_strat, phases, CAP, edge // phases, edge), ratings.dtype),
            pltpu.VMEM((n_strat, meta_rows, edge), jnp.int32),
            pltpu.VMEM((phases, n_rep * rows // phases, width), jnp.float32),
            pltpu.VMEM((phases, n_rep * rows // phases, width), jnp.bfloat16),
            pltpu.VMEM((n_strat, CAP * edge, edge), jnp.bfloat16),
            pltpu.VMEM((n_strat, CAP * edge, width), jnp.bfloat16),
            pltpu.VMEM((rows, width), jnp.float32),
            pltpu.VMEM((n_rep - 2, rows, width), jnp.bfloat16),
            pltpu.VMEM((n_strat, CAP, edge, edge), jnp.float32),
            pltpu.VMEM((n_strat, CAP, edge, edge), jnp.float32),
            pltpu.VMEM((n_strat, CAP * edge, width), jnp.bfloat16),
            dma((4,)),
            dma((4,)),
            dma((n_rep - 1,)),
            dma((n_rep - 1,)),
            dma((n_strat - 1, phases)),
            dma((n_strat - 1, phases)),
            dma((n_strat - 1,)),
            dma((n_strat - 1,)),
            dma((turns,)),
            dma((turns,)),
            dma((turns * (n_rep - 2),)),
            dma((n_rep - 2, turns)),
            pltpu.SemaphoreType.REGULAR,
            pltpu.SemaphoreType.REGULAR((n_strat,)),
        ],
        compiler_params=pltpu.CompilerParams(
            collective_id=0, has_side_effects=True
        ),
        name="gradient_pass",
    )(tile_owner.reshape(-1), tile_row, tile_col, tile_count, ratings, row_mask, row_factors, col_factors)
    row_grad, col_grad = (
        pltpu.with_memory_space_constraint(x, pltpu.VMEM) for x in (row_grad, col_grad)
    )
    anywhere = pl.BlockSpec(memory_space=pl.ANY)
    return pl.pallas_call(
        finish,
        out_shape=(
            jax.ShapeDtypeStruct((rows, width), jnp.float32),
            jax.ShapeDtypeStruct((cols, width), jnp.float32),
        ),
        in_specs=[anywhere] * 2,
        out_specs=(anywhere,) * 2,
        scratch_shapes=[dma((2,))],
        name="finish",
    )(row_grad, col_grad)


def solution(mesh):
    return jax.shard_map(
        on_device,
        mesh=mesh,
        in_specs=(
            P(("strat", "rep"), None, None),
            P(("strat", "rep"), None),
            P(("strat", "rep"), None),
            P(("strat", "rep")),
            P(("strat", "rep")),
            P(("strat", "rep")),
            P(("strat", "rep"), None),
            P(("strat", "rep"), None),
        ),
        out_specs=(P(("strat", "rep"), None), P(("strat", "rep"), None)),
        check_vma=False,
    )
```
